32 devices in a mesh: grp: 2 (over y), atoms: 4 (over z), feat: 2 (over x), rep: 2 (over core).
Axes of the slice: x: 2, y: 2, z: 4, core: 2. Of those that a mesh axis runs over, the one named last changes fastest.
Arguments:
- atom_coords: bfloat16 [4, 2048, 3, 3072], P(('grp', 'rep'), None, None, 'atoms'), parts along dimension 0, may hold values from -9 to 9
- atom_pairs: int32 [2, 1024], P(None, 'feat'), may hold values from 0 to 3071, as said below
- traj_ids: int32 [4, 2048], P(('grp', 'rep')), parts along dimension 0, may hold values from 0 to 7, never falling along the last dimension, each value on 1 to 512 neighbouring positions
Outputs:
- corr_inst: float32 [2048, 1024], P(('grp', 'atoms', 'rep'), 'feat'), parts along dimension 0
- corr_lag: float32 [2048, 1024], P(('grp', 'atoms', 'rep'), 'feat'), parts along dimension 0
- projections: float32 [4, 2048, 1024], P(('grp', 'rep'), 'atoms', 'feat'), parts along dimension 0
The draws below stay inside these ranges and needn't reach their ends.
There are 2 independent parts, one for each index of `grp`. The reference program is written for one: setup_inputs(seed, part) draws one part's arguments, and reference() takes and returns one part's arrays. A program takes and returns all parts, laid end to end along the dimension named above; an argument that names none is the same for every part. Nothing has to cross between parts.
Inputs may be any that keep to these rules, and one draw needn't show every extreme that they name: `atom_pairs`: the two atoms of a feature differ. `traj_ids`: trajectory numbers never fall along a replica stream; some trajectory holds exactly 512 frames.
All inputs are finite; a program needn't handle non-finite values.
Results may differ from the reference program's by a relative error of at most 0.0003.
Values may be sent and summed in bfloat16 or wider, within the bound.
A program may use at most 128 MiB of HBM per device.

```python
import math
import jax
import jax.numpy as jnp
import numpy as np
from jax import lax

ATOMS = 3072
FEATS = 1024
LAG = 10
TRAJS = 8
REPLICAS = 2
FRAMES = 2048


def draw_atom_coords(key, part):
    keys = jax.random.split(key, 10)
    base = jax.random.uniform(keys[0], (1, 1, 3, ATOMS), jnp.float32, -5.0, 5.0)
    times = jnp.arange(FRAMES, dtype=jnp.float32).reshape(1, FRAMES, 1, 1)
    envelope = 0.5 + times / FRAMES
    periods = jnp.exp(jax.random.uniform(keys[1], (3,), jnp.float32, math.log(40.0), math.log(400.0)))
    amplitudes = jax.random.uniform(keys[2], (3, 1, 1, 3, ATOMS), jnp.float32, 0.05, 0.35)
    phases = jax.random.uniform(keys[3], (3, REPLICAS, 1, 3, ATOMS), jnp.float32, -math.pi, math.pi)
    motion = jnp.zeros((REPLICAS, FRAMES, 3, ATOMS), jnp.float32)
    for mode in range(3):
        motion = motion + amplitudes[mode] * jnp.sin(2.0 * math.pi * times / periods[mode] + phases[mode])
    own_periods = jnp.exp(jax.random.uniform(keys[7], (1, 1, 3, ATOMS), jnp.float32, math.log(40.0), math.log(400.0)))
    own_amps = jnp.exp(jax.random.uniform(keys[8], (1, 1, 3, ATOMS), jnp.float32, math.log(0.3), math.log(0.8)))
    own_phases = jax.random.uniform(keys[9], (REPLICAS, 1, 3, ATOMS), jnp.float32, -math.pi, math.pi)
    own_motion = own_amps * jnp.sin(2.0 * math.pi * times / own_periods + own_phases)
    spread = jnp.exp(jax.random.uniform(keys[4], (1, 1, 1, ATOMS), jnp.float32, math.log(0.05), math.log(0.3)))
    noise = jax.random.truncated_normal(keys[6], -3.0, 3.0, (REPLICAS, FRAMES, 3, ATOMS), jnp.float32) * spread
    return (base + envelope * motion + own_motion + noise).astype(jnp.bfloat16)


def draw_atom_pairs(key, part):
    keys = jax.random.split(key, 2)
    first = jax.random.randint(keys[0], (FEATS,), 0, ATOMS, jnp.int32)
    first = first.at[0].set(ATOMS - 1).at[1].set(0)
    offset = jax.random.randint(keys[1], (FEATS,), 1, ATOMS, jnp.int32)
    second = (first + offset) % ATOMS
    return jnp.stack([first, second]).astype(jnp.int32)


def split_up(amount, total, most, skew):
    weights = [(1 << 20) // math.isqrt(rank ** skew) + 1 for rank in range(2, amount + 1)]
    surplus, counts = total - most - (amount - 1), [1] * (amount - 1)
    while surplus > 0:
        movable = [i for i in range(amount - 1) if counts[i] < most]
        whole, budget = sum([weights[i] for i in movable]), surplus
        for i in movable:
            extra = min(most - counts[i], max(1, budget * weights[i] // whole), surplus)
            counts[i] = counts[i] + extra
            surplus = surplus - extra
    return np.array([most] + counts)


def ragged(own_key, amount, total, most, skew):
    if amount == 2:
        one = jax.random.randint(own_key, (), max(1, total - most), min(most, total - 1) + 1)
        return jnp.stack([one, total - one])
    tallies = jnp.asarray(split_up(amount, total, most, skew), jnp.int32)
    twos = (amount - 1) // 2
    source_of, taker = tallies[1:1 + 2 * twos:2], tallies[2:2 + 2 * twos:2]
    margin = jnp.minimum(source_of - 1, most - taker)
    shifted = jax.random.randint(jax.random.fold_in(own_key, 1), (twos,), 0, 1 << 20) % (margin + 1)
    tallies = tallies.at[1:1 + 2 * twos:2].set(source_of - shifted).at[2:2 + 2 * twos:2].set(taker + shifted)
    return tallies[jax.random.permutation(jax.random.fold_in(own_key, 2), amount)]


def setup_inputs(seed: int = 0, part: int = 0) -> dict:
    arg_keys = jax.random.split(jax.random.key(seed), 4)
    own_keys = jax.random.split(jax.random.fold_in(arg_keys[3], part), 4)
    return {
        "atom_coords": draw_atom_coords(jax.random.fold_in(jax.random.fold_in(arg_keys[3], part), 71), part),
        "atom_pairs": draw_atom_pairs(jax.random.fold_in(arg_keys[3], 71), part),
        "traj_ids": jax.vmap(lambda own: jnp.searchsorted(jnp.cumsum(ragged(own, TRAJS, FRAMES, FRAMES // 4, 1)), jnp.arange(FRAMES), side="right"))(jax.random.split(own_keys[2], REPLICAS)).reshape((REPLICAS, FRAMES)).astype(jnp.int32),
    }


def featurize(positions, pairs):
    first = jnp.take(positions, pairs[0], axis=2)
    second = jnp.take(positions, pairs[1], axis=2)
    delta = first - second
    return jnp.sqrt(lax.optimization_barrier(jnp.sum(delta * delta, axis=1)) + 0.01)

def cross_moment(left, right):
    return lax.dot_general(left, right, (((0,), (0,)), ((), ())), precision=lax.Precision.HIGHEST, preferred_element_type=jnp.float32)

def reference(atom_coords, atom_pairs, traj_ids):
    padding = jnp.full((LAG,), -1, jnp.int32)
    present_list = []
    future_list = []
    valid_list = []
    for replica in range(REPLICAS):
        positions = atom_coords[replica].astype(jnp.float32)
        current = featurize(positions, atom_pairs)
        future = jnp.concatenate([current[LAG:], jnp.zeros((LAG, FEATS), jnp.float32)], 0)
        ids = jnp.concatenate([traj_ids[replica].astype(jnp.int32), padding])
        valid = (ids[:FRAMES] == ids[LAG:]).astype(jnp.float32)[:, None]
        present_list.append(current)
        future_list.append(future)
        valid_list.append(valid)
    count = jnp.float32(0.0)
    total_now = jnp.zeros((FEATS,), jnp.float32)
    total_next = jnp.zeros((FEATS,), jnp.float32)
    for replica in range(REPLICAS):
        count = count + jnp.sum(valid_list[replica])
        total_now = total_now + lax.optimization_barrier(jnp.sum(valid_list[replica] * present_list[replica], 0))
        total_next = total_next + lax.optimization_barrier(jnp.sum(valid_list[replica] * future_list[replica], 0))
    mean_now = total_now / count
    mean_next = total_next / count
    moment_inst = jnp.zeros((FEATS, FEATS), jnp.float32)
    moment_lag = jnp.zeros((FEATS, FEATS), jnp.float32)
    spread_now = jnp.zeros((FEATS,), jnp.float32)
    spread_next = jnp.zeros((FEATS,), jnp.float32)
    centered_list = []
    for replica in range(REPLICAS):
        centered = present_list[replica] - mean_now
        future_centered = future_list[replica] - mean_next
        valid = valid_list[replica]
        moment_inst = moment_inst + cross_moment(centered, valid * centered)
        moment_lag = moment_lag + cross_moment(centered, valid * future_centered)
        spread_now = spread_now + lax.optimization_barrier(jnp.sum(valid * centered * centered, 0))
        spread_next = spread_next + lax.optimization_barrier(jnp.sum(valid * future_centered * future_centered, 0))
        centered_list.append(centered)
    scale_now = 1.0 / jnp.sqrt(spread_now / count + 1e-05)
    scale_next = 1.0 / jnp.sqrt(spread_next / count + 1e-05)
    corr_inst = moment_inst / count * scale_now[:, None] * scale_now[None, :]
    corr_lag = moment_lag / count * scale_now[:, None] * scale_next[None, :]
    projections = jnp.stack([centered * scale_now for centered in centered_list])
    return (corr_inst, corr_lag, projections)
```

```python
import functools
import math

import jax
import jax.numpy as jnp
from jax import lax
from jax.experimental import pallas as pl
from jax.experimental.pallas import tpu as pltpu
from jax.sharding import PartitionSpec as P

LAG = 10
HALO = 16
CODE = 32700.0


def matmul(left, right, dims, precision=None):
    return lax.dot_general(
        left, right, (dims, ((), ())), precision=precision, preferred_element_type=jnp.float32
    )

MESH = pl.DeviceIdType.MESH


def exchange_kernel(
    groups, feat_groups, room, lanes, chunks, tile, coords, picked, slots, out, halo, *scratch
):
    blocks, pick, chosen, sign, recv, edge, load, z_send, z_recv, z_own, x_send, x_recv, h_send, h_recv = scratch
    z, x = lax.axis_index("atoms"), lax.axis_index("feat")
    half = groups // 2
    z_steps = [half] + [o for o in range(groups - 1, 0, -1) if o != half] if groups > 1 else []
    x_steps = list(range(1, feat_groups))
    tiles = out.shape[0] // tile
    frames_here = feat_groups * chunks * lanes
    cols = halo.shape[1]
    z_dests = [lax.rem(z + o, groups) for o in z_steps] + [z]
    loads = []
    for ch in range(chunks):
        row = []
        for i, dest in enumerate(z_dests):
            start = pl.multiple_of(dest * frames_here + (x * chunks + ch) * lanes, 16)
            row.append(
                pltpu.make_async_copy(coords.at[:, pl.ds(start, lanes), :], blocks.at[ch, i], load.at[ch, i])
            )
            row[-1].start()
        loads.append(row)
    barrier = pltpu.get_barrier_semaphore()
    for o in z_steps:
        pl.semaphore_signal(barrier, 1, device_id={"atoms": lax.rem(z + o, groups)}, device_id_type=MESH)
    for o in x_steps:
        pl.semaphore_signal(barrier, 1, device_id={"feat": lax.rem(x + o, feat_groups)}, device_id_type=MESH)
    z_up, z_down = lax.rem(z + 1, groups), lax.rem(z + groups - 1, groups)

    @pl.when(x == 0)
    def _():
        for k in x_steps:
            pl.semaphore_signal(barrier, 1, device_id={"atoms": z_down, "feat": k}, device_id_type=MESH)

    @pl.when(x != 0)
    def _():
        pl.semaphore_signal(barrier, 1, device_id={"atoms": z_up, "feat": 0}, device_id_type=MESH)

    width = picked.shape[1]
    slot_no = lax.broadcasted_iota(jnp.int32, (room, width), 0)
    pick[...] = jnp.where(slot_no == picked[...], 1.0, 0.0).astype(jnp.bfloat16)

    @pl.when(x == 0)
    def _():
        pl.semaphore_wait(barrier, len(z_steps) + 2 * len(x_steps))

    @pl.when(x != 0)
    def _():
        pl.semaphore_wait(barrier, len(z_steps) + len(x_steps) + 1)

    def fill(ch, i):
        loads[ch][i].wait()
        for c in range(3):
            got = lax.dot_general(
                pick[...], blocks[ch, i, c], (((1,), (1,)), ((), ())), preferred_element_type=jnp.float32
            )
            chosen[ch, i, :, c * lanes : (c + 1) * lanes] = got.astype(jnp.bfloat16)

    here = pl.ds(pl.multiple_of(z * room, 16), room)
    z_copies = []
    for ch in range(chunks):
        row = []
        for i, o in enumerate(z_steps):
            fill(ch, i)
            row.append(
                pltpu.make_async_remote_copy(
                    src_ref=chosen.at[ch, i],
                    dst_ref=recv.at[ch, here],
                    send_sem=z_send.at[ch, i],
                    recv_sem=z_recv.at[ch, i],
                    device_id={"atoms": z_dests[i]},
                    device_id_type=MESH,
                )
            )
            row[-1].start()
        z_copies.append(row)
    own_copies = []
    for ch in range(chunks):
        fill(ch, len(z_steps))
        own_copies.append(
            pltpu.make_async_copy(chosen.at[ch, len(z_steps)], recv.at[ch, here], z_own.at[ch])
        )
        own_copies[-1].start()

    place = lax.broadcasted_iota(jnp.int32, (128, groups * room), 1)

    def make_sign(i, carry):
        rows = pl.ds(pl.multiple_of(i * 128, 128), 128)
        pair = slots[rows, :]
        value = jnp.where(place == pair[:, 0:1], 1.0, 0.0) - jnp.where(place == pair[:, 1:2], 1.0, 0.0)
        sign[rows, :] = value.astype(jnp.bfloat16)
        return carry

    lax.fori_loop(0, out.shape[0] // 128, make_sign, 0)

    def x_copy(ch, i, k, o):
        part = out.at[
            pl.ds(pl.multiple_of(i * tile, tile), tile),
            pl.ds(pl.multiple_of((x * chunks + ch) * lanes, lanes), lanes),
        ]
        return pltpu.make_async_remote_copy(
            src_ref=part,
            dst_ref=part,
            send_sem=x_send.at[ch, i, k],
            recv_sem=x_recv.at[ch, i, k],
            device_id={"feat": lax.rem(x + o, feat_groups)},
            device_id_type=MESH,
        )

    def h_copy(k):
        return pltpu.make_async_remote_copy(
            src_ref=edge.at[:, k * cols : (k + 1) * cols],
            dst_ref=halo,
            send_sem=h_send.at[k],
            recv_sem=h_recv.at[0],
            device_id={"atoms": z_down, "feat": k},
            device_id_type=MESH,
        )

    for ch in range(chunks):
        own_copies[ch].wait()
        for copy in z_copies[ch]:
            copy.wait_recv()

        def features(i, carry, ch=ch):
            rows = pl.ds(pl.multiple_of(i * tile, tile), tile)
            delta = jnp.dot(sign[rows, :], recv[ch], preferred_element_type=jnp.float32)
            square = delta * delta
            total = square[:, :lanes] + square[:, lanes : 2 * lanes] + square[:, 2 * lanes :]
            cols = pl.ds(pl.multiple_of((x * chunks + ch) * lanes, lanes), lanes)
            out[rows, cols] = jnp.sqrt(total + 0.01)
            for k, o in enumerate(x_steps):
                x_copy(ch, i, k, o).start()
            return carry

        lax.fori_loop(0, tiles, features, 0)
        if ch == 0:

            @pl.when(x == 0)
            def _():
                for i in range(tiles):
                    first = out[i * tile : (i + 1) * tile, :lanes]
                    edge[:, i * tile : (i + 1) * tile] = first.T[:HALO]
                for k in range(feat_groups):
                    h_copy(k).start()

    @pl.when(x == 0)
    def _():
        for k in range(feat_groups):
            h_copy(k).wait_send()

    h_copy(0).wait_recv()
    for ch in range(chunks):
        for copy in z_copies[ch]:
            copy.wait_send()

        def finish(i, carry, ch=ch):
            for k, o in enumerate(x_steps):
                x_copy(ch, i, k, o).wait()
            return carry

        lax.fori_loop(0, tiles, finish, 0)


def exchange(coords, picked, slots, room, lanes, groups, feat_groups):
    feats, width = slots.shape[0], picked.shape[1]
    chunks = coords.shape[1] // (groups * feat_groups * lanes)
    tile = min(256, feats)
    vmem = pl.BlockSpec(memory_space=pltpu.VMEM)
    z_count, x_count = max(groups - 1, 1), max(feat_groups - 1, 1)
    dma = pltpu.SemaphoreType.DMA
    return pl.pallas_call(
        functools.partial(exchange_kernel, groups, feat_groups, room, lanes, chunks, tile),
        out_shape=(
            jax.ShapeDtypeStruct((feats, feat_groups * chunks * lanes), jnp.float32),
            jax.ShapeDtypeStruct((HALO, feats // feat_groups), jnp.float32),
        ),
        in_specs=[pl.BlockSpec(memory_space=pl.ANY), vmem, vmem],
        out_specs=(vmem, vmem),
        scratch_shapes=[
            pltpu.VMEM((chunks, groups, 3, lanes, width), jnp.bfloat16),
            pltpu.VMEM((room, width), jnp.bfloat16),
            pltpu.VMEM((chunks, groups, room, 3 * lanes), jnp.bfloat16),
            pltpu.VMEM((feats, groups * room), jnp.bfloat16),
            pltpu.VMEM((chunks, groups * room, 3 * lanes), jnp.bfloat16),
            pltpu.VMEM((HALO, feats), jnp.float32),
            dma((chunks, groups)),
            dma((chunks, z_count)),
            dma((chunks, z_count)),
            dma((chunks,)),
            dma((chunks, feats // tile, x_count)),
            dma((chunks, feats // tile, x_count)),
            dma((feat_groups,)),
            dma((1,)),
        ],
        compiler_params=pltpu.CompilerParams(
            collective_id=0, has_side_effects=True, vmem_limit_bytes=48 * 1024 * 1024
        ),
    )(coords, picked, slots)


def encode(inst, lag):
    def one(v):
        root = v * lax.rsqrt(jnp.abs(v) + 1e-30)
        return jnp.round(root * CODE).astype(jnp.int32)

    return (one(inst) << 16) | (one(lag) & 0xFFFF)


def decode(word):
    def one(q):
        root = q.astype(jnp.float32) * (1.0 / CODE)
        return root * jnp.abs(root)

    return one(word >> 16), one((word << 16) >> 16)


def split(value):
    high = value.astype(jnp.bfloat16)
    return high, (value - high.astype(jnp.float32)).astype(jnp.bfloat16)


def moments_kernel(
    groups, reps, every, halo, ids, inst, lag, proj, ext, vcol, left3, right3, local, core, stats, gathered,
    table, side, columns, scales, sums, from_below, from_above, *sems
):
    c_send, c_recv, s_own, s_send, s_recv, z_send, l_recv, r_recv = sems
    z, r, x = lax.axis_index("atoms"), lax.axis_index("rep"), lax.axis_index("feat")
    frames, feats = every.shape
    cols = halo.shape[1]
    rows = inst.shape[0]
    blocks = groups * reps
    me = z * reps + r
    peers = [(a, b) for a in range(groups) for b in range(reps) if (a, b) != (0, 0)]
    barrier = pltpu.get_barrier_semaphore()

    def peer(a, b):
        return {"atoms": lax.rem(z + a, groups), "rep": lax.rem(r + b, reps)}

    for a, b in peers:
        pl.semaphore_signal(barrier, 1, device_id=peer(a, b), device_id_type=MESH)

    here = ids[:, pl.ds(pl.multiple_of(z * frames, 128), frames)]
    after = ids[:, pl.ds(pl.multiple_of(jnp.minimum(z + 1, groups - 1) * frames, 128), 128)]
    after = jnp.where(z == groups - 1, -1, after)
    names = jnp.concatenate([here, after], 1).astype(jnp.float32)
    names = jnp.broadcast_to(names, (8, frames + 128))
    later = pltpu.roll(names, frames + 128 - LAG, 1)
    valid = (names == later).astype(jnp.float32)[:, :frames]
    count = jnp.sum(valid[:1], axis=1, keepdims=True)
    inverse = 1.0 / jnp.maximum(count, 1.0)
    vcol[...] = valid.T

    own = pl.ds(pl.multiple_of(x * cols, 128), cols)
    ext[:frames, :] = every[:, own]
    ext[frames:, :] = halo[...]
    step = 32

    def moved(i):
        wide = ext[pl.ds(pl.multiple_of(i * step, step), step + 16), :]
        return pltpu.roll(wide, step + 16 - LAG, 0)[:step]

    def fold(value):
        return jnp.sum(value.reshape(step // 8, 8, value.shape[1]), 0)

    def first(i, carry):
        at = pl.ds(pl.multiple_of(i * step, step), step)
        weight = vcol[at, :1]
        return carry[0] + fold(every[at, :] * weight), carry[1] + fold(moved(i) * weight)

    zero = (jnp.zeros((8, feats), jnp.float32), jnp.zeros((8, cols), jnp.float32))
    now_sum, next_sum = lax.fori_loop(0, frames // step, first, zero)
    now_mean = jnp.sum(now_sum, 0, keepdims=True) * inverse
    next_mean = jnp.sum(next_sum, 0, keepdims=True) * inverse

    def second(i, carry):
        base = pl.multiple_of(i * step, step)
        at, at1, at2 = pl.ds(base, step), pl.ds(base + frames, step), pl.ds(base + 2 * frames, step)
        weight = vcol[at, :1]
        now = (every[at, :] - now_mean) * weight
        later = (moved(i) - next_mean) * weight
        high, low = split(now)
        left3[at, :] = high
        left3[at1, :] = high
        left3[at2, :] = low
        right3[at, :cols] = left3[at, own]
        right3[at1, :cols] = left3[at2, own]
        right3[at2, :cols] = left3[at, own]
        high, low = split(later)
        right3[at, cols:] = high
        right3[at1, cols:] = low
        right3[at2, cols:] = high
        return carry[0] + fold(now * now), carry[1] + fold(later * later)

    now_sq, next_sq = lax.fori_loop(0, frames // step, second, zero)
    stats[...] = jnp.zeros_like(stats)
    stats[0:1, :] = now_mean
    stats[1:2, :] = jnp.sum(now_sq, 0, keepdims=True)
    stats[2:3, :cols] = next_mean
    stats[3:4, :cols] = jnp.sum(next_sq, 0, keepdims=True)
    stats[4:5, :] = jnp.broadcast_to(count, (1, feats))
    pl.semaphore_wait(barrier, len(peers))

    own_stats = pltpu.make_async_copy(stats, gathered.at[me], s_own.at[0])
    own_stats.start()
    stat_copies = []
    for k, (a, b) in enumerate(peers):
        stat_copies.append(
            pltpu.make_async_remote_copy(
                src_ref=stats,
                dst_ref=gathered.at[me],
                send_sem=s_send.at[k],
                recv_sem=s_recv.at[k],
                device_id=peer(a, b),
                device_id_type=MESH,
            )
        )
        stat_copies[-1].start()

    def core_copy(d, b):
        return pltpu.make_async_remote_copy(
            src_ref=local.at[d, lax.rem(r + b, reps)],
            dst_ref=core.at[b - 1, d],
            send_sem=c_send.at[b - 1, d],
            recv_sem=c_recv.at[b - 1, d],
            device_id={"rep": lax.rem(r + b, reps)},
            device_id_type=MESH,
        )

    tile = max(128, reps * rows)
    tiles, inside = feats // tile, tile // (reps * rows)

    def product(k, carry):
        half = k // 2
        t = jnp.where(k % 2 == 0, tiles - 1 - half, half)
        at = pl.ds(pl.multiple_of(t * tile, tile), tile)
        got = lax.dot_general(
            left3[:, at], right3[...], (((0,), (0,)), ((), ())), preferred_element_type=jnp.float32
        )
        for j in range(inside):
            d = t * inside + j
            for b in range(reps):
                low = (j * reps + b) * rows
                local[d, b] = got[low : low + rows]
            for b in range(1, reps):
                core_copy(d, b).start()
        return carry

    lax.fori_loop(0, tiles, product, 0)

    own_stats.wait()
    for copy in stat_copies:
        copy.wait()

    total = jnp.zeros((1, feats), jnp.float32)
    now_total = jnp.zeros((1, feats), jnp.float32)
    next_total = jnp.zeros((1, cols), jnp.float32)
    for b in range(blocks):
        size = gathered[b, 4:5, :]
        total = total + size
        now_total = now_total + size * gathered[b, 0:1, :]
        next_total = next_total + size[:, :cols] * gathered[b, 2:3, :cols]
    mean_now = now_total / total
    mean_next = next_total / total[:, :cols]
    now_spread = jnp.zeros((1, feats), jnp.float32)
    next_spread = jnp.zeros((1, cols), jnp.float32)
    for b in range(blocks):
        size = gathered[b, 4:5, :]
        off = gathered[b, 0:1, :] - mean_now
        now_spread = now_spread + (gathered[b, 1:2, :] + size * off * off)
        off = gathered[b, 2:3, :cols] - mean_next
        next_spread = next_spread + (gathered[b, 3:4, :cols] + size[:, :cols] * off * off)
    scale_now = 1.0 / jnp.sqrt(now_spread / total + 1e-05)
    scale_next = 1.0 / jnp.sqrt(next_spread / total[:, :cols] + 1e-05)
    root = 1.0 / jnp.sqrt(total)
    table[blocks : blocks + 1, :] = scale_now * root
    table[blocks + 1 : blocks + 2, :] = mean_now
    table[blocks + 2 : blocks + 3, :] = scale_now
    table[blocks + 3 :, :] = jnp.zeros((5, feats), jnp.float32)
    for b in range(blocks):
        size = gathered[b, 4:5, :]
        table[b : b + 1, :] = (gathered[b, 0:1, :] - mean_now) * (scale_now * root)
        side[b : b + 1, cols:] = (
            size[:, :cols] * (gathered[b, 2:3, :cols] - mean_next) * (scale_next * root[:, :cols])
        )
    for b in range(blocks):
        side[b : b + 1, :cols] = gathered[b, 4:5, :cols] * table[b : b + 1, own]
    scales[0:1, :cols] = table[blocks : blocks + 1, own]
    scales[0:1, cols:] = scale_next * root[:, :cols]
    columns[...] = table[...].T

    tall = min(rows, 32)

    def hop(d, up):
        return pltpu.make_async_remote_copy(
            src_ref=sums.at[d],
            dst_ref=(from_below if up else from_above).at[d],
            send_sem=z_send.at[d],
            recv_sem=(l_recv if up else r_recv).at[d],
            device_id={"atoms": lax.rem(z + (1 if up else groups - 1), groups)},
            device_id_type=MESH,
        )

    def mine(d, i):
        at = pl.ds(pl.multiple_of(i * tall, tall), tall)
        value = local[d, r, at, :]
        for b in range(1, reps):
            value = value + core[b - 1, d, at, :]
        high = pl.ds(pl.multiple_of((d * reps + r) * rows + i * tall, tall), tall)
        return value * columns[high, blocks : blocks + 1] * scales[0:1, :]

    def wait_core(d):
        for b in range(1, reps):
            core_copy(d, b).wait_recv()

    def send(d, up, relay):
        if relay:
            hop(d, up).wait_recv()

        def body(i, carry):
            at = pl.ds(pl.multiple_of(i * tall, tall), tall)
            value = mine(d, i)
            inst_part, lag_part = value[:, :cols], value[:, cols:]
            if relay:
                more = decode((from_below if up else from_above)[d, at, :])
                inst_part, lag_part = inst_part + more[0], lag_part + more[1]
            sums[d, at, :] = encode(inst_part, lag_part)
            return carry

        lax.fori_loop(0, rows // tall, body, 0)
        hop(d, up).start()

    def chain(k, carry):
        above, below = groups - 1 - k, k

        @pl.when(z < above)
        def _():
            wait_core(above)

            @pl.when(z == 0)
            def _():
                send(above, True, False)

            @pl.when(z > 0)
            def _():
                send(above, True, True)

        @pl.when(z > below)
        def _():
            wait_core(below)

            @pl.when(z == groups - 1)
            def _():
                send(below, False, False)

            @pl.when(z < groups - 1)
            def _():
                send(below, False, True)

        return carry

    lax.fori_loop(0, groups, chain, 0)

    wait_core(z)

    def settle(i, carry):
        at = pl.ds(pl.multiple_of(i * tall, tall), tall)
        high = pl.ds(pl.multiple_of(me * rows + i * tall, tall), tall)
        shift = lax.dot_general(
            columns[high, :blocks], side[...], (((1,), (0,)), ((), ())),
            precision=lax.Precision.HIGHEST, preferred_element_type=jnp.float32,
        )
        value = mine(z, i) + shift
        inst[at, :] = value[:, :cols]
        lag[at, :] = value[:, cols:]
        return carry

    lax.fori_loop(0, rows // tall, settle, 0)

    center, stretch = table[blocks + 1 : blocks + 2, own], table[blocks + 2 : blocks + 3, own]

    def project(i, carry):
        at = pl.ds(pl.multiple_of(i * step, step), step)
        proj[at, :] = (ext[at, :] - center) * stretch
        return carry

    lax.fori_loop(0, frames // step, project, 0)

    def arrive(up):
        hop(z, up).wait_recv()

        def body(i, carry):
            at = pl.ds(pl.multiple_of(i * tall, tall), tall)
            more = decode((from_below if up else from_above)[z, at, :])
            inst[at, :] = inst[at, :] + more[0]
            lag[at, :] = lag[at, :] + more[1]
            return carry

        lax.fori_loop(0, rows // tall, body, 0)

    @pl.when(z > 0)
    def _():
        arrive(True)

    @pl.when(z < groups - 1)
    def _():
        arrive(False)

    def finish(d, carry):
        for b in range(1, reps):
            core_copy(d, b).wait_send()

        @pl.when(z < d)
        def _():
            hop(d, True).wait_send()

        @pl.when(z > d)
        def _():
            hop(d, False).wait_send()

        return carry

    lax.fori_loop(0, groups, finish, 0)


def moments(every, halo, ids, groups, reps):
    frames, feats = every.shape
    cols = halo.shape[1]
    blocks = groups * reps
    rows = feats // blocks
    vmem = pl.BlockSpec(memory_space=pltpu.VMEM)
    dma = pltpu.SemaphoreType.DMA
    others, others_core = max(blocks - 1, 1), max(reps - 1, 1)
    word = pltpu.VMEM((groups, rows, cols), jnp.int32)
    return pl.pallas_call(
        functools.partial(moments_kernel, groups, reps),
        out_shape=(
            jax.ShapeDtypeStruct((rows, cols), jnp.float32),
            jax.ShapeDtypeStruct((rows, cols), jnp.float32),
            jax.ShapeDtypeStruct((frames, cols), jnp.float32),
        ),
        in_specs=[vmem, vmem, vmem],
        out_specs=(vmem, vmem, vmem),
        scratch_shapes=[
            pltpu.VMEM((frames + HALO, cols), jnp.float32),
            pltpu.VMEM((frames, 8), jnp.float32),
            pltpu.VMEM((3 * frames, feats), jnp.bfloat16),
            pltpu.VMEM((3 * frames, 2 * cols), jnp.bfloat16),
            pltpu.VMEM((groups, reps, rows, 2 * cols), jnp.float32),
            pltpu.VMEM((others_core, groups, rows, 2 * cols), jnp.float32),
            pltpu.VMEM((8, feats), jnp.float32),
            pltpu.VMEM((blocks, 8, feats), jnp.float32),
            pltpu.VMEM((blocks + 8, feats), jnp.float32),
            pltpu.VMEM((blocks, 2 * cols), jnp.float32),
            pltpu.VMEM((feats, blocks + 8), jnp.float32),
            pltpu.VMEM((8, 2 * cols), jnp.float32),
            word,
            word,
            word,
            dma((others_core, groups)),
            dma((others_core, groups)),
            dma((1,)),
            dma((others,)),
            dma((others,)),
            dma((groups,)),
            dma((groups,)),
            dma((groups,)),
        ],
        compiler_params=pltpu.CompilerParams(
            collective_id=1, has_side_effects=True, vmem_limit_bytes=56 * 1024 * 1024
        ),
    )(every, halo, ids)


def slots_per_pass(width, refs, atoms):
    share = width * (1.0 - math.exp(-refs / atoms)) + 2.05 * math.sqrt(width)
    return min(-(-width // 16) * 16, -(-int(share) // 16) * 16)


def shards(atom_coords, atom_pairs, traj_ids):
    groups = lax.axis_size("atoms")
    feat_groups = lax.axis_size("feat")
    frames = atom_coords.shape[1]
    frames_here = frames // groups
    part = frames_here // feat_groups
    width = atom_coords.shape[3]
    cols = atom_pairs.shape[1]
    z = lax.axis_index("atoms")
    x = lax.axis_index("feat")

    pairs = lax.all_gather(atom_pairs, "feat", axis=1, tiled=True)
    feats = pairs.shape[1]
    refs = pairs.reshape(-1)
    room = slots_per_pass(width, 2 * feats, width * groups)

    atom_no = jnp.arange(groups * width, dtype=jnp.int32).reshape(groups, width)
    hit = atom_no[:, :, None] == refs[None, None, :]
    used = jnp.any(hit, axis=2)
    before = (jnp.arange(width)[:, None] < jnp.arange(width)[None, :]).astype(jnp.bfloat16)
    rank = matmul(used.astype(jnp.bfloat16), before, ((1,), (0,)))
    most = jnp.max(jnp.sum(used.astype(jnp.float32), 1))
    ref_rank = jnp.sum(jnp.where(hit, rank[:, :, None], 0.0), axis=(0, 1)).reshape(2, feats)
    ref_shard = pairs // width
    used_own = lax.dynamic_index_in_dim(used, z, 0, False)
    rank_own = lax.dynamic_index_in_dim(rank, z, 0, False)

    coords = jnp.transpose(atom_coords[0], (1, 0, 2))
    lanes = 128 if part % 128 == 0 else part
    chunks = part // lanes

    def spots(turn):
        spot = ref_rank - turn * jnp.float32(room)
        inside = (spot >= 0) & (spot < room)
        return jnp.where(inside, ref_shard * room + spot.astype(jnp.int32), -1).T

    def one_pass():
        picked = jnp.where(used_own, rank_own.astype(jnp.int32), -1)[None]
        return exchange(coords, picked, spots(jnp.float32(0.0)), room, lanes, groups, feat_groups)

    def more_passes():
        def step(carry):
            turn, delta = carry
            spot = spots(turn)
            slot = jnp.arange(room, dtype=jnp.float32) + turn * jnp.float32(room)
            pick = ((rank_own[None, :] == slot[:, None]) & used_own[None, :]).astype(jnp.bfloat16)
            grouped = coords.reshape(3, groups, feat_groups, part, width)
            blocks = lax.dynamic_index_in_dim(grouped, x, 2, False)
            chosen = matmul(pick, blocks, ((1,), (3,))).astype(jnp.bfloat16)
            chosen = jnp.transpose(chosen.reshape(room, 3, groups, chunks, lanes), (2, 3, 0, 1, 4))
            chosen = chosen.reshape(groups, chunks, room, 3 * lanes)
            got = lax.all_to_all(chosen, "atoms", split_axis=0, concat_axis=0, tiled=True)
            got = jnp.transpose(got, (0, 2, 1, 3)).reshape(groups * room, chunks * 3 * lanes)
            place = jnp.arange(groups * room, dtype=jnp.int32)
            sign = (spot[:, :1] == place).astype(jnp.bfloat16) - (spot[:, 1:] == place).astype(jnp.bfloat16)
            return turn + 1.0, delta + matmul(sign, got, ((1,), (0,)))

        _, delta = lax.while_loop(
            lambda c: c[0] * room < most,
            step,
            (jnp.float32(0.0), jnp.zeros((feats, chunks * 3 * lanes), jnp.float32)),
        )
        delta = delta.reshape(feats, chunks, 3, lanes)
        computed = jnp.sqrt(jnp.sum(delta * delta, axis=2) + 0.01).reshape(feats, part)
        both = jnp.zeros((feats, frames_here), jnp.float32)
        for o in range(feat_groups):
            turned = lax.ppermute(computed, "feat", [(i, (i + o) % feat_groups) for i in range(feat_groups)])
            both = lax.dynamic_update_slice_in_dim(both, turned, ((x - o) % feat_groups) * part, 1)
        first = lax.dynamic_slice_in_dim(both[:, :HALO], x * cols, cols, 0).T
        return both, lax.ppermute(first, "atoms", [(i, (i - 1) % groups) for i in range(groups)])

    every, incoming = lax.cond(most <= room, one_pass, more_passes)
    corr_inst, corr_lag, projections = moments(every.T, incoming, traj_ids, groups, lax.axis_size("rep"))
    return (corr_inst, corr_lag, projections[None])


def solution(mesh):
    placed = (P(("grp", "rep"), None, None, "atoms"), P(None, "feat"), P(("grp", "rep"), None))
    return jax.shard_map(
        shards,
        mesh=mesh,
        in_specs=placed,
        out_specs=(
            P(("grp", "atoms", "rep"), "feat"),
            P(("grp", "atoms", "rep"), "feat"),
            P(("grp", "rep"), "atoms", "feat"),
        ),
        check_vma=False,
    )
```

```python
import functools
import math

import jax
import jax.numpy as jnp
from jax import lax
from jax.experimental import pallas as pl
from jax.experimental.pallas import tpu as pltpu
from jax.sharding import PartitionSpec as P

LAG = 10
HALO = 16
CODE = 32700.0


def matmul(left, right, dims, precision=None):
    return lax.dot_general(
        left, right, (dims, ((), ())), precision=precision, preferred_element_type=jnp.float32
    )

MESH = pl.DeviceIdType.MESH


def exchange_kernel(groups, feat_groups, room, chunks, coords, pairs, every, halo, over, *scratch):
    (
        blocks, everyone, ranks, pick, front, back, sign, front_in, back_in, third,
        load, p_send, p_recv, f_send, f_recv, b_send, b_recv, f_own, b_own, x_send, x_recv, h_send, h_recv,
    ) = scratch
    z, x = lax.axis_index("atoms"), lax.axis_index("feat")
    lanes, part = 128, 64
    width = coords.shape[2]
    feats, cols = every.shape[1], pairs.shape[1]
    half = groups // 2
    z_steps = [half] + [o for o in range(groups - 1, 0, -1) if o != half] if groups > 1 else []
    x_steps = list(range(1, feat_groups))
    frames_here = feat_groups * chunks * lanes
    z_dests = [lax.rem(z + o, groups) for o in z_steps] + [z]
    loads = []
    for ch in range(chunks):
        row = []
        for i, dest in enumerate(z_dests):
            start = pl.multiple_of(dest * frames_here + (x * chunks + ch) * lanes, 16)
            row.append(
                pltpu.make_async_copy(coords.at[:, pl.ds(start, lanes), :], blocks.at[ch, i], load.at[ch, i])
            )
            row[-1].start()
        loads.append(row)
    barrier = pltpu.get_barrier_semaphore()
    for o in z_steps:
        pl.semaphore_signal(barrier, 1, device_id={"atoms": lax.rem(z + o, groups)}, device_id_type=MESH)
    for o in x_steps:
        pl.semaphore_signal(barrier, 1, device_id={"feat": lax.rem(x + o, feat_groups)}, device_id_type=MESH)
    z_up, z_down = lax.rem(z + 1, groups), lax.rem(z + groups - 1, groups)

    @pl.when(x == 0)
    def _():
        for k in x_steps:
            pl.semaphore_signal(barrier, 1, device_id={"atoms": z_down, "feat": k}, device_id_type=MESH)

    @pl.when(x != 0)
    def _():
        pl.semaphore_signal(barrier, 1, device_id={"atoms": z_up, "feat": 0}, device_id_type=MESH)

    everyone[x] = pairs[...]

    @pl.when(x == 0)
    def _():
        pl.semaphore_wait(barrier, len(z_steps) + 2 * len(x_steps))

    @pl.when(x != 0)
    def _():
        pl.semaphore_wait(barrier, len(z_steps) + len(x_steps) + 1)

    pair_copies = []
    for k, o in enumerate(x_steps):
        pair_copies.append(
            pltpu.make_async_remote_copy(
                src_ref=pairs,
                dst_ref=everyone.at[x],
                send_sem=p_send.at[k],
                recv_sem=p_recv.at[k],
                device_id={"feat": lax.rem(x + o, feat_groups)},
                device_id_type=MESH,
            )
        )
        pair_copies[-1].start()
    for copy in pair_copies:
        copy.wait()

    lines = -(-width // lanes)
    height = -(-groups * lines // 16) * 16

    def iota(shape, dim):
        return lax.broadcasted_iota(jnp.int32, shape, dim)

    def bins(value, size):
        return sum(((value >= s * size).astype(jnp.int32) for s in range(1, groups)), jnp.zeros_like(value))

    def ones(mask):
        return jnp.where(mask, 1.0, 0.0).astype(jnp.bfloat16)

    def product(a, b, dims):
        return lax.dot_general(a, b, (dims, ((), ())), preferred_element_type=jnp.float32)

    found, counts = [], jnp.zeros((height, lanes), jnp.float32)
    for k in range(2):
        ref = jnp.concatenate([everyone[i, k : k + 1, :] for i in range(feat_groups)], 1)
        shard = bins(ref, width)
        inner = ref - shard * width
        line = ones(iota((height, feats), 0) == shard * lines + (inner >> 7))
        spot = ones(iota((lanes, feats), 0) == (inner & 127))
        counts = counts + product(line, spot, ((1,), (1,)))
        found.append((shard, line, spot))
    used = ones(counts > 0.5)
    earlier = ones(iota((lanes, lanes), 0) < iota((lanes, lanes), 1))
    row_shard, col_shard = bins(iota((height, height), 0), lines), bins(iota((height, height), 1), lines)
    same = row_shard == col_shard
    filled = product(used, jnp.ones((lanes, lanes), jnp.bfloat16), ((1,), (0,))).astype(jnp.bfloat16)
    before = product(
        ones(same & (iota((height, height), 1) < iota((height, height), 0))), filled, ((1,), (0,))
    )
    rank = product(used, earlier, ((1,), (0,))) + before
    most = jnp.max(product(ones(same), filled, ((1,), (0,))))
    over[...] = jnp.where(jnp.broadcast_to(most, over.shape) > room, 1.0, 0.0)
    ranks[...] = jnp.where(counts > 0.5, rank, -1.0)
    whole = rank.astype(jnp.int32)
    parts = jnp.concatenate(
        [(whole >> 4).astype(jnp.float32), (whole & 15).astype(jnp.float32)], 0
    ).astype(jnp.bfloat16)
    slots = []
    for shard, line, spot in found:
        got = product(parts, spot, ((1,), (0,)))
        chosen = (got[:height] * 16.0 + got[height:]) * line.astype(jnp.float32)
        place = jnp.sum(chosen, 0, keepdims=True).astype(jnp.int32)
        slots.append(jnp.where(place < room, shard * room + place, -1))

    slot_no = iota((room, lanes), 0).astype(jnp.float32)
    for j in range(lines):
        wide = min(lanes, width - j * lanes)
        row = ranks[pl.ds(z * lines + j, 1), :]
        pick[:, j * lanes : j * lanes + wide] = ones(slot_no == row)[:, :wide]

    def fill(ch, i):
        loads[ch][i].wait()

        def get(first):
            return product(pick[...], first, ((1,), (1,))).astype(jnp.bfloat16)

        early = [blocks[ch, i, c, :part] for c in range(2)]
        late = [blocks[ch, i, c, part:] for c in range(2)]
        front[ch, i, :, :lanes] = get(jnp.concatenate(early, 0))
        front[ch, i, :, lanes:] = get(blocks[ch, i, 2])
        back[ch, i] = get(jnp.concatenate(late, 0))

    here = pl.ds(pl.multiple_of(z * room, 16), room)

    def z_copy(source, target, send, recv, ch, i):
        return pltpu.make_async_remote_copy(
            src_ref=source.at[ch, i],
            dst_ref=target.at[ch, here],
            send_sem=send.at[ch, i],
            recv_sem=recv.at[ch, i],
            device_id={"atoms": z_dests[i]},
            device_id_type=MESH,
        )

    fronts, backs = [], []
    for ch in range(chunks):
        fronts.append([])
        backs.append([])
        for i in range(len(z_steps)):
            fill(ch, i)
            fronts[ch].append(z_copy(front, front_in, f_send, f_recv, ch, i))
            fronts[ch][i].start()
        for i in range(len(z_steps)):
            backs[ch].append(z_copy(back, back_in, b_send, b_recv, ch, i))
            backs[ch][i].start()
    last = len(z_steps)
    front_own, back_own = [], []
    for ch in range(chunks):
        fill(ch, last)
        front_own.append(pltpu.make_async_copy(front.at[ch, last], front_in.at[ch, here], f_own.at[ch]))
        back_own.append(pltpu.make_async_copy(back.at[ch, last], back_in.at[ch, here], b_own.at[ch]))
        front_own[ch].start()
        back_own[ch].start()

    def make_sign(i, carry):
        at = pl.ds(pl.multiple_of(i * 16, 16), 16)
        number = iota((16, feats), 0) + i * 16
        value = jnp.where(number == slots[0], 1.0, 0.0) - jnp.where(number == slots[1], 1.0, 0.0)
        sign[at, :] = value.astype(jnp.bfloat16)
        return carry

    lax.fori_loop(0, groups * room // 16, make_sign, 0)

    def x_copy(ch, p, k, o):
        at = every.at[pl.ds(pl.multiple_of((x * chunks + ch) * lanes + p * part, part), part), :]
        return pltpu.make_async_remote_copy(
            src_ref=at,
            dst_ref=at,
            send_sem=x_send.at[ch, p, k],
            recv_sem=x_recv.at[ch, p, k],
            device_id={"feat": lax.rem(x + o, feat_groups)},
            device_id_type=MESH,
        )

    def h_copy(k):
        return pltpu.make_async_remote_copy(
            src_ref=every.at[:HALO, k * cols : (k + 1) * cols],
            dst_ref=halo,
            send_sem=h_send.at[k],
            recv_sem=h_recv.at[0],
            device_id={"atoms": z_down, "feat": k},
            device_id_type=MESH,
        )

    def keep(ch, p, total):
        at = pl.ds(pl.multiple_of((x * chunks + ch) * lanes + p * part, part), part)
        every[at, :] = jnp.sqrt(total + 0.01)
        for k, o in enumerate(x_steps):
            x_copy(ch, p, k, o).start()

    for ch in range(chunks):
        front_own[ch].wait()
        for copy in fronts[ch]:
            copy.wait_recv()
        delta = product(front_in[ch], sign[...], ((0,), (0,)))
        square = delta * delta
        third[...] = square[3 * part :]
        keep(ch, 0, square[:part] + square[part : 2 * part] + square[2 * part : 3 * part])
        if ch == 0:

            @pl.when(x == 0)
            def _():
                for k in range(feat_groups):
                    h_copy(k).start()

        back_own[ch].wait()
        for copy in backs[ch]:
            copy.wait_recv()
        delta = product(back_in[ch], sign[...], ((0,), (0,)))
        square = delta * delta
        keep(ch, 1, square[:part] + square[part:] + third[...])

    @pl.when(x == 0)
    def _():
        for k in range(feat_groups):
            h_copy(k).wait_send()

    h_copy(0).wait_recv()
    for ch in range(chunks):
        for copy in fronts[ch] + backs[ch]:
            copy.wait_send()
        for p in range(2):
            for k, o in enumerate(x_steps):
                x_copy(ch, p, k, o).wait()


def exchange(coords, pairs, room, groups, feat_groups):
    cols, width = pairs.shape[1], coords.shape[2]
    feats = cols * feat_groups
    chunks = coords.shape[1] // (groups * feat_groups * 128)
    height = -(-groups * -(-width // 128) // 16) * 16
    vmem = pl.BlockSpec(memory_space=pltpu.VMEM)
    z_count, x_count = max(groups - 1, 1), max(feat_groups - 1, 1)
    dma = pltpu.SemaphoreType.DMA
    return pl.pallas_call(
        functools.partial(exchange_kernel, groups, feat_groups, room, chunks),
        out_shape=(
            jax.ShapeDtypeStruct((feat_groups * chunks * 128, feats), jnp.float32),
            jax.ShapeDtypeStruct((HALO, cols), jnp.float32),
            jax.ShapeDtypeStruct((8, 128), jnp.float32),
        ),
        in_specs=[pl.BlockSpec(memory_space=pl.ANY), vmem],
        out_specs=(vmem, vmem, vmem),
        scratch_shapes=[
            pltpu.VMEM((chunks, groups, 3, 128, width), jnp.bfloat16),
            pltpu.VMEM((feat_groups, 2, cols), jnp.int32),
            pltpu.VMEM((height, 128), jnp.float32),
            pltpu.VMEM((room, width), jnp.bfloat16),
            pltpu.VMEM((chunks, groups, room, 256), jnp.bfloat16),
            pltpu.VMEM((chunks, groups, room, 128), jnp.bfloat16),
            pltpu.VMEM((groups * room, feats), jnp.bfloat16),
            pltpu.VMEM((chunks, groups * room, 256), jnp.bfloat16),
            pltpu.VMEM((chunks, groups * room, 128), jnp.bfloat16),
            pltpu.VMEM((64, feats), jnp.float32),
            dma((chunks, groups)),
            dma((x_count,)),
            dma((x_count,)),
            dma((chunks, z_count)),
            dma((chunks, z_count)),
            dma((chunks, z_count)),
            dma((chunks, z_count)),
            dma((chunks,)),
            dma((chunks,)),
            dma((chunks, 2, x_count)),
            dma((chunks, 2, x_count)),
            dma((feat_groups,)),
            dma((1,)),
        ],
        compiler_params=pltpu.CompilerParams(
            collective_id=0, has_side_effects=True, vmem_limit_bytes=56 * 1024 * 1024
        ),
    )(coords, pairs)


def encode(inst, lag):
    def one(v):
        root = v * lax.rsqrt(jnp.abs(v) + 1e-30)
        return jnp.round(root * CODE).astype(jnp.int32)

    return (one(inst) << 16) | (one(lag) & 0xFFFF)


def decode(word):
    def one(q):
        root = q.astype(jnp.float32) * (1.0 / CODE)
        return root * jnp.abs(root)

    return one(word >> 16), one((word << 16) >> 16)


def split(value):
    high = value.astype(jnp.bfloat16)
    return high, (value - high.astype(jnp.float32)).astype(jnp.bfloat16)


def moments_kernel(
    groups, reps, every, halo, ids, inst, lag, proj, ext, vcol, left3, right3, local, core, stats, gathered,
    table, side, columns, scales, sums, from_below, from_above, *sems
):
    c_send, c_recv, s_own, s_send, s_recv, z_send, l_recv, r_recv = sems
    z, r, x = lax.axis_index("atoms"), lax.axis_index("rep"), lax.axis_index("feat")
    frames, feats = every.shape
    cols = halo.shape[1]
    rows = inst.shape[0]
    blocks = groups * reps
    me = z * reps + r
    peers = [(a, b) for a in range(groups) for b in range(reps) if (a, b) != (0, 0)]
    barrier = pltpu.get_barrier_semaphore()

    def peer(a, b):
        return {"atoms": lax.rem(z + a, groups), "rep": lax.rem(r + b, reps)}

    for a, b in peers:
        pl.semaphore_signal(barrier, 1, device_id=peer(a, b), device_id_type=MESH)

    here = ids[:, pl.ds(pl.multiple_of(z * frames, 128), frames)]
    after = ids[:, pl.ds(pl.multiple_of(jnp.minimum(z + 1, groups - 1) * frames, 128), 128)]
    after = jnp.where(z == groups - 1, -1, after)
    names = jnp.concatenate([here, after], 1).astype(jnp.float32)
    names = jnp.broadcast_to(names, (8, frames + 128))
    later = pltpu.roll(names, frames + 128 - LAG, 1)
    valid = (names == later).astype(jnp.float32)[:, :frames]
    count = jnp.sum(valid[:1], axis=1, keepdims=True)
    inverse = 1.0 / jnp.maximum(count, 1.0)
    vcol[...] = valid.T

    own = pl.ds(pl.multiple_of(x * cols, 128), cols)
    ext[:frames, :] = every[:, own]
    ext[frames:, :] = halo[...]
    step = 32

    def moved(i):
        wide = ext[pl.ds(pl.multiple_of(i * step, step), step + 16), :]
        return pltpu.roll(wide, step + 16 - LAG, 0)[:step]

    def fold(value):
        return jnp.sum(value.reshape(step // 8, 8, value.shape[1]), 0)

    def first(i, carry):
        at = pl.ds(pl.multiple_of(i * step, step), step)
        weight = vcol[at, :1]
        return carry[0] + fold(every[at, :] * weight), carry[1] + fold(moved(i) * weight)

    zero = (jnp.zeros((8, feats), jnp.float32), jnp.zeros((8, cols), jnp.float32))
    now_sum, next_sum = lax.fori_loop(0, frames // step, first, zero)
    now_mean = jnp.sum(now_sum, 0, keepdims=True) * inverse
    next_mean = jnp.sum(next_sum, 0, keepdims=True) * inverse

    def second(i, carry):
        base = pl.multiple_of(i * step, step)
        at, at1, at2 = pl.ds(base, step), pl.ds(base + frames, step), pl.ds(base + 2 * frames, step)
        weight = vcol[at, :1]
        now = (every[at, :] - now_mean) * weight
        later = (moved(i) - next_mean) * weight
        high, low = split(now)
        left3[at, :] = high
        left3[at1, :] = high
        left3[at2, :] = low
        right3[at, :cols] = left3[at, own]
        right3[at1, :cols] = left3[at2, own]
        right3[at2, :cols] = left3[at, own]
        high, low = split(later)
        right3[at, cols:] = high
        right3[at1, cols:] = low
        right3[at2, cols:] = high
        return carry[0] + fold(now * now), carry[1] + fold(later * later)

    now_sq, next_sq = lax.fori_loop(0, frames // step, second, zero)
    stats[...] = jnp.zeros_like(stats)
    stats[0:1, :] = now_mean
    stats[1:2, :] = jnp.sum(now_sq, 0, keepdims=True)
    stats[2:3, :cols] = next_mean
    stats[3:4, :cols] = jnp.sum(next_sq, 0, keepdims=True)
    stats[4:5, :] = jnp.broadcast_to(count, (1, feats))
    pl.semaphore_wait(barrier, len(peers))

    own_stats = pltpu.make_async_copy(stats, gathered.at[me], s_own.at[0])
    own_stats.start()
    stat_copies = []
    for k, (a, b) in enumerate(peers):
        stat_copies.append(
            pltpu.make_async_remote_copy(
                src_ref=stats,
                dst_ref=gathered.at[me],
                send_sem=s_send.at[k],
                recv_sem=s_recv.at[k],
                device_id=peer(a, b),
                device_id_type=MESH,
            )
        )
        stat_copies[-1].start()

    def core_copy(d, b):
        return pltpu.make_async_remote_copy(
            src_ref=local.at[d, lax.rem(r + b, reps)],
            dst_ref=core.at[b - 1, d],
            send_sem=c_send.at[b - 1, d],
            recv_sem=c_recv.at[b - 1, d],
            device_id={"rep": lax.rem(r + b, reps)},
            device_id_type=MESH,
        )

    tile = max(128, reps * rows)
    tiles, inside = feats // tile, tile // (reps * rows)

    def product(k, carry):
        half = k // 2
        t = jnp.where(k % 2 == 0, tiles - 1 - half, half)
        at = pl.ds(pl.multiple_of(t * tile, tile), tile)
        got = lax.dot_general(
            left3[:, at], right3[...], (((0,), (0,)), ((), ())), preferred_element_type=jnp.float32
        )
        for j in range(inside):
            d = t * inside + j
            for b in range(reps):
                low = (j * reps + b) * rows
                local[d, b] = got[low : low + rows]
            for b in range(1, reps):
                core_copy(d, b).start()
        return carry

    lax.fori_loop(0, tiles, product, 0)

    own_stats.wait()
    for copy in stat_copies:
        copy.wait()

    total = jnp.zeros((1, feats), jnp.float32)
    now_total = jnp.zeros((1, feats), jnp.float32)
    next_total = jnp.zeros((1, cols), jnp.float32)
    for b in range(blocks):
        size = gathered[b, 4:5, :]
        total = total + size
        now_total = now_total + size * gathered[b, 0:1, :]
        next_total = next_total + size[:, :cols] * gathered[b, 2:3, :cols]
    mean_now = now_total / total
    mean_next = next_total / total[:, :cols]
    now_spread = jnp.zeros((1, feats), jnp.float32)
    next_spread = jnp.zeros((1, cols), jnp.float32)
    for b in range(blocks):
        size = gathered[b, 4:5, :]
        off = gathered[b, 0:1, :] - mean_now
        now_spread = now_spread + (gathered[b, 1:2, :] + size * off * off)
        off = gathered[b, 2:3, :cols] - mean_next
        next_spread = next_spread + (gathered[b, 3:4, :cols] + size[:, :cols] * off * off)
    scale_now = 1.0 / jnp.sqrt(now_spread / total + 1e-05)
    scale_next = 1.0 / jnp.sqrt(next_spread / total[:, :cols] + 1e-05)
    root = 1.0 / jnp.sqrt(total)
    table[blocks : blocks + 1, :] = scale_now * root
    table[blocks + 1 : blocks + 2, :] = mean_now
    table[blocks + 2 : blocks + 3, :] = scale_now
    table[blocks + 3 :, :] = jnp.zeros((5, feats), jnp.float32)
    for b in range(blocks):
        size = gathered[b, 4:5, :]
        table[b : b + 1, :] = (gathered[b, 0:1, :] - mean_now) * (scale_now * root)
        side[b : b + 1, cols:] = (
            size[:, :cols] * (gathered[b, 2:3, :cols] - mean_next) * (scale_next * root[:, :cols])
        )
    for b in range(blocks):
        side[b : b + 1, :cols] = gathered[b, 4:5, :cols] * table[b : b + 1, own]
    scales[0:1, :cols] = table[blocks : blocks + 1, own]
    scales[0:1, cols:] = scale_next * root[:, :cols]
    columns[...] = table[...].T

    tall = min(rows, 32)

    def hop(d, up):
        return pltpu.make_async_remote_copy(
            src_ref=sums.at[d],
            dst_ref=(from_below if up else from_above).at[d],
            send_sem=z_send.at[d],
            recv_sem=(l_recv if up else r_recv).at[d],
            device_id={"atoms": lax.rem(z + (1 if up else groups - 1), groups)},
            device_id_type=MESH,
        )

    def mine(d, i):
        at = pl.ds(pl.multiple_of(i * tall, tall), tall)
        value = local[d, r, at, :]
        for b in range(1, reps):
            value = value + core[b - 1, d, at, :]
        high = pl.ds(pl.multiple_of((d * reps + r) * rows + i * tall, tall), tall)
        return value * columns[high, blocks : blocks + 1] * scales[0:1, :]

    def wait_core(d):
        for b in range(1, reps):
            core_copy(d, b).wait_recv()

    def send(d, up, relay):
        if relay:
            hop(d, up).wait_recv()

        def body(i, carry):
            at = pl.ds(pl.multiple_of(i * tall, tall), tall)
            value = mine(d, i)
            inst_part, lag_part = value[:, :cols], value[:, cols:]
            if relay:
                more = decode((from_below if up else from_above)[d, at, :])
                inst_part, lag_part = inst_part + more[0], lag_part + more[1]
            sums[d, at, :] = encode(inst_part, lag_part)
            return carry

        lax.fori_loop(0, rows // tall, body, 0)
        hop(d, up).start()

    def chain(k, carry):
        above, below = groups - 1 - k, k

        @pl.when(z < above)
        def _():
            wait_core(above)

            @pl.when(z == 0)
            def _():
                send(above, True, False)

            @pl.when(z > 0)
            def _():
                send(above, True, True)

        @pl.when(z > below)
        def _():
            wait_core(below)

            @pl.when(z == groups - 1)
            def _():
                send(below, False, False)

            @pl.when(z < groups - 1)
            def _():
                send(below, False, True)

        return carry

    lax.fori_loop(0, groups, chain, 0)

    wait_core(z)

    def settle(i, carry):
        at = pl.ds(pl.multiple_of(i * tall, tall), tall)
        high = pl.ds(pl.multiple_of(me * rows + i * tall, tall), tall)
        shift = lax.dot_general(
            columns[high, :blocks], side[...], (((1,), (0,)), ((), ())),
            precision=lax.Precision.HIGHEST, preferred_element_type=jnp.float32,
        )
        value = mine(z, i) + shift
        inst[at, :] = value[:, :cols]
        lag[at, :] = value[:, cols:]
        return carry

    lax.fori_loop(0, rows // tall, settle, 0)

    center, stretch = table[blocks + 1 : blocks + 2, own], table[blocks + 2 : blocks + 3, own]

    def project(i, carry):
        at = pl.ds(pl.multiple_of(i * step, step), step)
        proj[at, :] = (ext[at, :] - center) * stretch
        return carry

    lax.fori_loop(0, frames // step, project, 0)

    def arrive(up):
        hop(z, up).wait_recv()

        def body(i, carry):
            at = pl.ds(pl.multiple_of(i * tall, tall), tall)
            more = decode((from_below if up else from_above)[z, at, :])
            inst[at, :] = inst[at, :] + more[0]
            lag[at, :] = lag[at, :] + more[1]
            return carry

        lax.fori_loop(0, rows // tall, body, 0)

    @pl.when(z > 0)
    def _():
        arrive(True)

    @pl.when(z < groups - 1)
    def _():
        arrive(False)

    def finish(d, carry):
        for b in range(1, reps):
            core_copy(d, b).wait_send()

        @pl.when(z < d)
        def _():
            hop(d, True).wait_send()

        @pl.when(z > d)
        def _():
            hop(d, False).wait_send()

        return carry

    lax.fori_loop(0, groups, finish, 0)


def moments(every, halo, ids, groups, reps):
    frames, feats = every.shape
    cols = halo.shape[1]
    blocks = groups * reps
    rows = feats // blocks
    vmem = pl.BlockSpec(memory_space=pltpu.VMEM)
    dma = pltpu.SemaphoreType.DMA
    others, others_core = max(blocks - 1, 1), max(reps - 1, 1)
    word = pltpu.VMEM((groups, rows, cols), jnp.int32)
    return pl.pallas_call(
        functools.partial(moments_kernel, groups, reps),
        out_shape=(
            jax.ShapeDtypeStruct((rows, cols), jnp.float32),
            jax.ShapeDtypeStruct((rows, cols), jnp.float32),
            jax.ShapeDtypeStruct((frames, cols), jnp.float32),
        ),
        in_specs=[vmem, vmem, vmem],
        out_specs=(vmem, vmem, vmem),
        scratch_shapes=[
            pltpu.VMEM((frames + HALO, cols), jnp.float32),
            pltpu.VMEM((frames, 8), jnp.float32),
            pltpu.VMEM((3 * frames, feats), jnp.bfloat16),
            pltpu.VMEM((3 * frames, 2 * cols), jnp.bfloat16),
            pltpu.VMEM((groups, reps, rows, 2 * cols), jnp.float32),
            pltpu.VMEM((others_core, groups, rows, 2 * cols), jnp.float32),
            pltpu.VMEM((8, feats), jnp.float32),
            pltpu.VMEM((blocks, 8, feats), jnp.float32),
            pltpu.VMEM((blocks + 8, feats), jnp.float32),
            pltpu.VMEM((blocks, 2 * cols), jnp.float32),
            pltpu.VMEM((feats, blocks + 8), jnp.float32),
            pltpu.VMEM((8, 2 * cols), jnp.float32),
            word,
            word,
            word,
            dma((others_core, groups)),
            dma((others_core, groups)),
            dma((1,)),
            dma((others,)),
            dma((others,)),
            dma((groups,)),
            dma((groups,)),
            dma((groups,)),
        ],
        compiler_params=pltpu.CompilerParams(
            collective_id=1, has_side_effects=True, vmem_limit_bytes=56 * 1024 * 1024
        ),
    )(every, halo, ids)


def write_kernel(*refs):
    count = len(refs) // 2
    ins, outs, sem = refs[:count], refs[count:-1], refs[-1]
    copies = [pltpu.make_async_copy(a, b, sem.at[i]) for i, (a, b) in enumerate(zip(ins, outs))]
    for copy in copies:
        copy.start()
    for copy in copies:
        copy.wait()


def write_out(*arrays):
    vmem, anywhere = pl.BlockSpec(memory_space=pltpu.VMEM), pl.BlockSpec(memory_space=pl.ANY)
    return pl.pallas_call(
        write_kernel,
        out_shape=tuple(jax.ShapeDtypeStruct(a.shape, a.dtype) for a in arrays),
        in_specs=[vmem] * len(arrays),
        out_specs=(anywhere,) * len(arrays),
        scratch_shapes=[pltpu.SemaphoreType.DMA((len(arrays),))],
    )(*arrays)


def slots_per_pass(width, refs, atoms):
    share = width * (1.0 - math.exp(-refs / atoms)) + 2.05 * math.sqrt(width)
    return min(-(-width // 16) * 16, -(-int(share) // 16) * 16)


def collect(value, axis):
    size = lax.axis_size(axis)
    return lax.all_to_all(jnp.broadcast_to(value[None], (size,) + value.shape), axis, 0, 0, tiled=True)


def plain(coords, atom_pairs, traj_ids):
    groups, feat_groups, reps = lax.axis_size("atoms"), lax.axis_size("feat"), lax.axis_size("rep")
    z, x = lax.axis_index("atoms"), lax.axis_index("feat")
    width, cols = coords.shape[2], atom_pairs.shape[1]
    frames = coords.shape[1] // groups
    feats = cols * feat_groups
    exact = lax.Precision.HIGHEST

    split_up = jnp.transpose(coords.reshape(3, groups, frames, width), (1, 0, 2, 3))
    got = lax.all_to_all(split_up, "atoms", 0, 0, tiled=True)
    number = jnp.arange(groups * width, dtype=jnp.int32)[:, None]
    sign = (number == atom_pairs[0]).astype(jnp.bfloat16) - (number == atom_pairs[1]).astype(jnp.bfloat16)
    delta = matmul(got, sign.reshape(groups, width, cols), ((0, 3), (0, 1)))
    own = jnp.sqrt(jnp.sum(delta * delta, 0) + 0.01)
    every = jnp.transpose(collect(own, "feat"), (1, 0, 2)).reshape(frames, feats)
    incoming = lax.ppermute(own[:LAG], "atoms", [(i, (i - 1) % groups) for i in range(groups)])
    future = jnp.concatenate([own[LAG:], incoming], 0)
    ids = jnp.concatenate([traj_ids[0], jnp.full((LAG,), -1, jnp.int32)])
    now = lax.dynamic_slice_in_dim(ids, z * frames, frames)
    later = lax.dynamic_slice_in_dim(ids, z * frames + LAG, frames)
    valid = (now == later).astype(jnp.float32)[:, None]

    def total(value):
        return jnp.sum(collect(jnp.sum(collect(value, "rep"), 0), "atoms"), 0)

    count = total(jnp.full((128,), jnp.sum(valid)))[0]
    mean_now = total(jnp.sum(valid * every, 0)) / count
    mean_next = total(jnp.sum(valid * future, 0)) / count
    now_c, next_c = valid * (every - mean_now), valid * (future - mean_next)
    scale_now = 1.0 / jnp.sqrt(total(jnp.sum(now_c * now_c, 0)) / count + 1e-05)
    scale_next = 1.0 / jnp.sqrt(total(jnp.sum(next_c * next_c, 0)) / count + 1e-05)
    own_c = lax.dynamic_slice_in_dim(now_c, x * cols, cols, 1)
    own_scale = lax.dynamic_slice_in_dim(scale_now, x * cols, cols)
    own_mean = lax.dynamic_slice_in_dim(mean_now, x * cols, cols)
    local = matmul(now_c, jnp.concatenate([own_c, next_c], 1), ((0,), (0,)), exact)
    rows = feats // (groups * reps)
    local = local.reshape(groups, reps, rows, 2 * cols)
    local = jnp.sum(lax.all_to_all(local, "atoms", 0, 0, tiled=True), 0)
    mine = jnp.sum(lax.all_to_all(local, "rep", 0, 0, tiled=True), 0)
    row = (z * reps + lax.axis_index("rep")) * rows
    scale_rows = lax.dynamic_slice_in_dim(scale_now, row, rows)[:, None]
    corr_inst = mine[:, :cols] / count * scale_rows * own_scale
    corr_lag = mine[:, cols:] / count * scale_rows * scale_next
    return corr_inst, corr_lag, (own - own_mean) * own_scale


def shards(atom_coords, atom_pairs, traj_ids):
    groups, feat_groups, reps = lax.axis_size("atoms"), lax.axis_size("feat"), lax.axis_size("rep")
    width = atom_coords.shape[3]
    room = slots_per_pass(width, 2 * atom_pairs.shape[1] * feat_groups, width * groups)
    coords = jnp.transpose(atom_coords[0], (1, 0, 2))
    every, halo, over = exchange(coords, atom_pairs, room, groups, feat_groups)
    results = moments(every, halo, traj_ids, groups, reps)
    corr_inst, corr_lag, projections = lax.cond(
        over[0, 0] > 0.0,
        lambda a: plain(coords, atom_pairs, traj_ids),
        lambda a: write_out(*a),
        results,
    )
    return (corr_inst, corr_lag, projections[None])


def solution(mesh):
    placed = (P(("grp", "rep"), None, None, "atoms"), P(None, "feat"), P(("grp", "rep"), None))
    return jax.shard_map(
        shards,
        mesh=mesh,
        in_specs=placed,
        out_specs=(
            P(("grp", "atoms", "rep"), "feat"),
            P(("grp", "atoms", "rep"), "feat"),
            P(("grp", "rep"), "atoms", "feat"),
        ),
        check_vma=False,
    )
```

```python
import functools
import math

import jax
import jax.numpy as jnp
from jax import lax
from jax.experimental import pallas as pl
from jax.experimental.pallas import tpu as pltpu
from jax.sharding import PartitionSpec as P

LAG = 10
HALO = 16
CODE = 32700.0
PIECES = 2


def matmul(left, right, dims, precision=None):
    return lax.dot_general(
        left, right, (dims, ((), ())), precision=precision, preferred_element_type=jnp.float32
    )

MESH = pl.DeviceIdType.MESH


def program_kernel(groups, feat_groups, reps, room, chunks, coords, pairs, ids, inst, lag, proj, over, *scratch):
    (
        every, halo, blocks_in, everyone, ranks, pick, front, back, sign, front_in, back_in, third,
        ext, vcol, left3, right3, local, core, stats, gathered, table, side, columns, scales,
        sums, from_below, from_above,
        load, p_send, p_recv, f_send, f_recv, b_send, b_recv, f_own, b_own, x_send, x_recv, h_send, h_recv,
        c_send, c_recv, s_own, s_send, s_recv, z_send, l_recv, r_recv,
    ) = scratch
    z, r, x = lax.axis_index("atoms"), lax.axis_index("rep"), lax.axis_index("feat")
    peers = [(a, b) for a in range(groups) for b in range(reps) if (a, b) != (0, 0)]
    lanes, part = 128, 64
    width = coords.shape[2]
    feats, cols = every.shape[1], pairs.shape[1]
    half = groups // 2
    z_steps = [half] + [o for o in range(groups - 1, 0, -1) if o != half] if groups > 1 else []
    x_steps = list(range(1, feat_groups))
    frames_here = feat_groups * chunks * lanes
    z_dests = [lax.rem(z + o, groups) for o in z_steps] + [z]
    loads = []
    for ch in range(chunks):
        row = []
        for i, dest in enumerate(z_dests):
            start = pl.multiple_of(dest * frames_here + (x * chunks + ch) * lanes, 16)
            row.append(
                pltpu.make_async_copy(coords.at[:, pl.ds(start, lanes), :], blocks_in.at[ch, i], load.at[ch, i])
            )
            row[-1].start()
        loads.append(row)
    barrier = pltpu.get_barrier_semaphore()

    def peer(a, b):
        return {"atoms": lax.rem(z + a, groups), "rep": lax.rem(r + b, reps)}

    for a, b in peers:
        pl.semaphore_signal(barrier, 1, device_id=peer(a, b), device_id_type=MESH)
    for o in x_steps:
        pl.semaphore_signal(barrier, 1, device_id={"feat": lax.rem(x + o, feat_groups)}, device_id_type=MESH)
    z_up, z_down = lax.rem(z + 1, groups), lax.rem(z + groups - 1, groups)

    @pl.when(x == 0)
    def _():
        for k in x_steps:
            pl.semaphore_signal(barrier, 1, device_id={"atoms": z_down, "feat": k}, device_id_type=MESH)

    @pl.when(x != 0)
    def _():
        pl.semaphore_signal(barrier, 1, device_id={"atoms": z_up, "feat": 0}, device_id_type=MESH)

    everyone[x] = pairs[...]

    @pl.when(x == 0)
    def _():
        pl.semaphore_wait(barrier, len(peers) + 2 * len(x_steps))

    @pl.when(x != 0)
    def _():
        pl.semaphore_wait(barrier, len(peers) + len(x_steps) + 1)

    pair_copies = []
    for k, o in enumerate(x_steps):
        pair_copies.append(
            pltpu.make_async_remote_copy(
                src_ref=pairs,
                dst_ref=everyone.at[x],
                send_sem=p_send.at[k],
                recv_sem=p_recv.at[k],
                device_id={"feat": lax.rem(x + o, feat_groups)},
                device_id_type=MESH,
            )
        )
        pair_copies[-1].start()
    for copy in pair_copies:
        copy.wait()

    lines = -(-width // lanes)
    height = -(-groups * lines // 16) * 16

    def iota(shape, dim):
        return lax.broadcasted_iota(jnp.int32, shape, dim)

    def bins(value, size):
        return sum(((value >= s * size).astype(jnp.int32) for s in range(1, groups)), jnp.zeros_like(value))

    def ones(mask):
        return jnp.where(mask, 1.0, 0.0).astype(jnp.bfloat16)

    def product(a, b, dims):
        return lax.dot_general(a, b, (dims, ((), ())), preferred_element_type=jnp.float32)

    found, counts = [], jnp.zeros((height, lanes), jnp.float32)
    for k in range(2):
        ref = jnp.concatenate([everyone[i, k : k + 1, :] for i in range(feat_groups)], 1)
        shard = bins(ref, width)
        inner = ref - shard * width
        line = ones(iota((height, feats), 0) == shard * lines + (inner >> 7))
        spot = ones(iota((lanes, feats), 0) == (inner & 127))
        counts = counts + product(line, spot, ((1,), (1,)))
        found.append((shard, line, spot))
    used = ones(counts > 0.5)
    earlier = ones(iota((lanes, lanes), 0) < iota((lanes, lanes), 1))
    row_shard, col_shard = bins(iota((height, height), 0), lines), bins(iota((height, height), 1), lines)
    same = row_shard == col_shard
    filled = product(used, jnp.ones((lanes, lanes), jnp.bfloat16), ((1,), (0,))).astype(jnp.bfloat16)
    before = product(
        ones(same & (iota((height, height), 1) < iota((height, height), 0))), filled, ((1,), (0,))
    )
    rank = product(used, earlier, ((1,), (0,))) + before
    most = jnp.max(product(ones(same), filled, ((1,), (0,))))
    over[0, 0] = most
    ranks[...] = jnp.where(counts > 0.5, rank, -1.0)
    whole = rank.astype(jnp.int32)
    parts = jnp.concatenate(
        [(whole >> 4).astype(jnp.float32), (whole & 15).astype(jnp.float32)], 0
    ).astype(jnp.bfloat16)
    slots = []
    for shard, line, spot in found:
        got = product(parts, spot, ((1,), (0,)))
        chosen = (got[:height] * 16.0 + got[height:]) * line.astype(jnp.float32)
        place = jnp.sum(chosen, 0, keepdims=True).astype(jnp.int32)
        slots.append(jnp.where(place < room, shard * room + place, -1))

    slot_no = iota((room, lanes), 0).astype(jnp.float32)
    for j in range(lines):
        wide = min(lanes, width - j * lanes)
        row = ranks[pl.ds(z * lines + j, 1), :]
        pick[:, j * lanes : j * lanes + wide] = ones(slot_no == row)[:, :wide]

    def fill(ch, i):
        loads[ch][i].wait()

        def get(first):
            return product(pick[...], first, ((1,), (1,))).astype(jnp.bfloat16)

        early = [blocks_in[ch, i, c, :part] for c in range(2)]
        late = [blocks_in[ch, i, c, part:] for c in range(2)]
        front[ch, i, :, :lanes] = get(jnp.concatenate(early, 0))
        front[ch, i, :, lanes:] = get(blocks_in[ch, i, 2])
        back[ch, i] = get(jnp.concatenate(late, 0))

    here = pl.ds(pl.multiple_of(z * room, 16), room)

    def z_copy(source, target, send, recv, ch, i):
        return pltpu.make_async_remote_copy(
            src_ref=source.at[ch, i],
            dst_ref=target.at[ch, here],
            send_sem=send.at[ch, i],
            recv_sem=recv.at[ch, i],
            device_id={"atoms": z_dests[i]},
            device_id_type=MESH,
        )

    fronts, backs = [], []
    for ch in range(chunks):
        fronts.append([])
        backs.append([])
        for i in range(len(z_steps)):
            fill(ch, i)
            fronts[ch].append(z_copy(front, front_in, f_send, f_recv, ch, i))
            fronts[ch][i].start()
        for i in range(len(z_steps)):
            backs[ch].append(z_copy(back, back_in, b_send, b_recv, ch, i))
            backs[ch][i].start()
    last = len(z_steps)
    front_own, back_own = [], []
    for ch in range(chunks):
        fill(ch, last)
        front_own.append(pltpu.make_async_copy(front.at[ch, last], front_in.at[ch, here], f_own.at[ch]))
        back_own.append(pltpu.make_async_copy(back.at[ch, last], back_in.at[ch, here], b_own.at[ch]))
        front_own[ch].start()
        back_own[ch].start()

    def make_sign(i, carry):
        at = pl.ds(pl.multiple_of(i * 16, 16), 16)
        number = iota((16, feats), 0) + i * 16
        value = jnp.where(number == slots[0], 1.0, 0.0) - jnp.where(number == slots[1], 1.0, 0.0)
        sign[at, :] = value.astype(jnp.bfloat16)
        return carry

    lax.fori_loop(0, groups * room // 16, make_sign, 0)

    def x_copy(ch, p, k, o):
        at = every.at[pl.ds(pl.multiple_of((x * chunks + ch) * lanes + p * part, part), part), :]
        return pltpu.make_async_remote_copy(
            src_ref=at,
            dst_ref=at,
            send_sem=x_send.at[ch, p, k],
            recv_sem=x_recv.at[ch, p, k],
            device_id={"feat": lax.rem(x + o, feat_groups)},
            device_id_type=MESH,
        )

    def h_copy(k):
        return pltpu.make_async_remote_copy(
            src_ref=every.at[:HALO, k * cols : (k + 1) * cols],
            dst_ref=halo,
            send_sem=h_send.at[k],
            recv_sem=h_recv.at[0],
            device_id={"atoms": z_down, "feat": k},
            device_id_type=MESH,
        )

    def keep(ch, p, total):
        at = pl.ds(pl.multiple_of((x * chunks + ch) * lanes + p * part, part), part)
        every[at, :] = jnp.sqrt(total + 0.01)
        for k, o in enumerate(x_steps):
            x_copy(ch, p, k, o).start()

    for ch in range(chunks):
        front_own[ch].wait()
        for copy in fronts[ch]:
            copy.wait_recv()
        delta = product(front_in[ch], sign[...], ((0,), (0,)))
        square = delta * delta
        third[...] = square[3 * part :]
        keep(ch, 0, square[:part] + square[part : 2 * part] + square[2 * part : 3 * part])
        if ch == 0:

            @pl.when(x == 0)
            def _():
                for k in range(feat_groups):
                    h_copy(k).start()

        back_own[ch].wait()
        for copy in backs[ch]:
            copy.wait_recv()
        delta = product(back_in[ch], sign[...], ((0,), (0,)))
        square = delta * delta
        keep(ch, 1, square[:part] + square[part:] + third[...])

    h_copy(0).wait_recv()
    for ch in range(chunks):
        for p in range(2):
            for k, o in enumerate(x_steps):
                x_copy(ch, p, k, o).wait_recv()

    frames, rows, blocks = frames_here, inst.shape[0], groups * reps
    me = z * reps + r
    present = ids[:, pl.ds(pl.multiple_of(z * frames, 128), frames)]
    after = ids[:, pl.ds(pl.multiple_of(jnp.minimum(z + 1, groups - 1) * frames, 128), 128)]
    after = jnp.where(z == groups - 1, -1, after)
    names = jnp.concatenate([present, after], 1).astype(jnp.float32)
    names = jnp.broadcast_to(names, (8, frames + 128))
    later = pltpu.roll(names, frames + 128 - LAG, 1)
    valid = (names == later).astype(jnp.float32)[:, :frames]
    count = jnp.sum(valid[:1], axis=1, keepdims=True)
    inverse = 1.0 / jnp.maximum(count, 1.0)
    vcol[...] = valid.T

    own = pl.ds(pl.multiple_of(x * cols, 128), cols)
    ext[:frames, :] = every[:, own]
    ext[frames:, :] = halo[...]
    step = 32

    def moved(i):
        wide = ext[pl.ds(pl.multiple_of(i * step, step), step + 16), :]
        return pltpu.roll(wide, step + 16 - LAG, 0)[:step]

    def fold(value):
        return jnp.sum(value.reshape(step // 8, 8, value.shape[1]), 0)

    def first(i, carry):
        at = pl.ds(pl.multiple_of(i * step, step), step)
        weight = vcol[at, :1]
        return carry[0] + fold(every[at, :] * weight), carry[1] + fold(moved(i) * weight)

    zero = (jnp.zeros((8, feats), jnp.float32), jnp.zeros((8, cols), jnp.float32))
    now_sum, next_sum = lax.fori_loop(0, frames // step, first, zero)
    now_mean = jnp.sum(now_sum, 0, keepdims=True) * inverse
    next_mean = jnp.sum(next_sum, 0, keepdims=True) * inverse

    def second(i, carry):
        base = pl.multiple_of(i * step, step)
        at, at1, at2 = pl.ds(base, step), pl.ds(base + frames, step), pl.ds(base + 2 * frames, step)
        weight = vcol[at, :1]
        now = (every[at, :] - now_mean) * weight
        later = (moved(i) - next_mean) * weight
        high, low = split(now)
        left3[at, :] = high
        left3[at1, :] = high
        left3[at2, :] = low
        right3[at, :cols] = left3[at, own]
        right3[at1, :cols] = left3[at2, own]
        right3[at2, :cols] = left3[at, own]
        high, low = split(later)
        right3[at, cols:] = high
        right3[at1, cols:] = low
        right3[at2, cols:] = high
        return carry[0] + fold(now * now), carry[1] + fold(later * later)

    now_sq, next_sq = lax.fori_loop(0, frames // step, second, zero)
    stats[0:1, :] = now_mean
    stats[1:2, :] = jnp.sum(now_sq, 0, keepdims=True)
    stats[2:3, :cols] = next_mean
    stats[2:3, cols : 2 * cols] = jnp.sum(next_sq, 0, keepdims=True)
    stats[3:4, :feats] = jnp.broadcast_to(count, (1, feats))

    own_stats = pltpu.make_async_copy(stats, gathered.at[me], s_own.at[0])
    own_stats.start()
    stat_copies = []
    for k, (a, b) in enumerate(peers):
        stat_copies.append(
            pltpu.make_async_remote_copy(
                src_ref=stats,
                dst_ref=gathered.at[me],
                send_sem=s_send.at[k],
                recv_sem=s_recv.at[k],
                device_id=peer(a, b),
                device_id_type=MESH,
            )
        )
        stat_copies[-1].start()

    def core_copy(d, b):
        return pltpu.make_async_remote_copy(
            src_ref=local.at[d, lax.rem(r + b, reps)],
            dst_ref=core.at[b - 1, d],
            send_sem=c_send.at[b - 1, d],
            recv_sem=c_recv.at[b - 1, d],
            device_id={"rep": lax.rem(r + b, reps)},
            device_id_type=MESH,
        )

    tile = max(128, reps * rows)
    tiles, inside = feats // tile, tile // (reps * rows)

    def multiply(k, carry):
        half = k // 2
        t = jnp.where(k % 2 == 0, tiles - 1 - half, half)
        at = pl.ds(pl.multiple_of(t * tile, tile), tile)
        got = lax.dot_general(
            left3[:, at], right3[...], (((0,), (0,)), ((), ())), preferred_element_type=jnp.float32
        )
        for j in range(inside):
            d = t * inside + j
            for b in range(reps):
                low = (j * reps + b) * rows
                local[d, b] = got[low : low + rows]
            for b in range(1, reps):
                core_copy(d, b).start()
        return carry

    lax.fori_loop(0, tiles, multiply, 0)

    own_stats.wait()
    for copy in stat_copies:
        copy.wait()

    total = jnp.zeros((1, feats), jnp.float32)
    now_total = jnp.zeros((1, feats), jnp.float32)
    next_total = jnp.zeros((1, cols), jnp.float32)
    for b in range(blocks):
        size = gathered[b, 3:4, :feats]
        total = total + size
        now_total = now_total + size * gathered[b, 0:1, :feats]
        next_total = next_total + size[:, :cols] * gathered[b, 2:3, :cols]
    mean_now = now_total / total
    mean_next = next_total / total[:, :cols]
    now_spread = jnp.zeros((1, feats), jnp.float32)
    next_spread = jnp.zeros((1, cols), jnp.float32)
    for b in range(blocks):
        size = gathered[b, 3:4, :feats]
        off = gathered[b, 0:1, :feats] - mean_now
        now_spread = now_spread + (gathered[b, 1:2, :feats] + size * off * off)
        off = gathered[b, 2:3, :cols] - mean_next
        next_spread = next_spread + (gathered[b, 2:3, cols : 2 * cols] + size[:, :cols] * off * off)
    scale_now = 1.0 / jnp.sqrt(now_spread / total + 1e-05)
    scale_next = 1.0 / jnp.sqrt(next_spread / total[:, :cols] + 1e-05)
    root = 1.0 / jnp.sqrt(total)
    table[blocks : blocks + 1, :] = scale_now * root
    table[blocks + 1 : blocks + 2, :] = mean_now
    table[blocks + 2 : blocks + 3, :] = scale_now
    table[blocks + 3 :, :] = jnp.zeros((5, feats), jnp.float32)
    for b in range(blocks):
        size = gathered[b, 3:4, :feats]
        table[b : b + 1, :] = (gathered[b, 0:1, :feats] - mean_now) * (scale_now * root)
        side[b : b + 1, cols:] = (
            size[:, :cols] * (gathered[b, 2:3, :cols] - mean_next) * (scale_next * root[:, :cols])
        )
    for b in range(blocks):
        side[b : b + 1, :cols] = gathered[b, 3:4, :cols] * table[b : b + 1, own]
    scales[0:1, :cols] = table[blocks : blocks + 1, own]
    scales[0:1, cols:] = scale_next * root[:, :cols]
    columns[...] = table[...].T

    tall = min(rows // PIECES, 32)
    piece = rows // PIECES

    def hop(d, s, up):
        at = pl.ds(pl.multiple_of(s * piece, piece), piece)
        return pltpu.make_async_remote_copy(
            src_ref=sums.at[d, at],
            dst_ref=(from_below if up else from_above).at[d, at],
            send_sem=z_send.at[d, s],
            recv_sem=(l_recv if up else r_recv).at[d, s],
            device_id={"atoms": lax.rem(z + (1 if up else groups - 1), groups)},
            device_id_type=MESH,
        )

    def mine(d, i):
        at = pl.ds(pl.multiple_of(i * tall, tall), tall)
        value = local[d, r, at, :]
        for b in range(1, reps):
            value = value + core[b - 1, d, at, :]
        high = pl.ds(pl.multiple_of((d * reps + r) * rows + i * tall, tall), tall)
        return value * columns[high, blocks : blocks + 1] * scales[0:1, :]

    def wait_core(d):
        for b in range(1, reps):
            core_copy(d, b).wait_recv()

    def send(d, s, up, relay):
        if relay:
            hop(d, s, up).wait_recv()

        def body(j, carry):
            i = s * (piece // tall) + j
            at = pl.ds(pl.multiple_of(i * tall, tall), tall)
            value = mine(d, i)
            inst_part, lag_part = value[:, :cols], value[:, cols:]
            if relay:
                more = decode((from_below if up else from_above)[d, at, :])
                inst_part, lag_part = inst_part + more[0], lag_part + more[1]
            sums[d, at, :] = encode(inst_part, lag_part)
            return carry

        lax.fori_loop(0, piece // tall, body, 0)
        hop(d, s, up).start()

    def chain(k, carry):
        below, s = k // PIECES, k % PIECES
        above = groups - 1 - below

        @pl.when(z < above)
        def _():
            @pl.when(s == 0)
            def _():
                wait_core(above)

            @pl.when(z == 0)
            def _():
                send(above, s, True, False)

            @pl.when(z > 0)
            def _():
                send(above, s, True, True)

        @pl.when(z > below)
        def _():
            @pl.when(s == 0)
            def _():
                wait_core(below)

            @pl.when(z == groups - 1)
            def _():
                send(below, s, False, False)

            @pl.when(z < groups - 1)
            def _():
                send(below, s, False, True)

        return carry

    lax.fori_loop(0, groups * PIECES, chain, 0)

    wait_core(z)

    def settle(i, carry):
        at = pl.ds(pl.multiple_of(i * tall, tall), tall)
        high = pl.ds(pl.multiple_of(me * rows + i * tall, tall), tall)
        shift = lax.dot_general(
            columns[high, :blocks], side[...], (((1,), (0,)), ((), ())),
            precision=lax.Precision.HIGHEST, preferred_element_type=jnp.float32,
        )
        value = mine(z, i) + shift
        inst[at, :] = value[:, :cols]
        lag[at, :] = value[:, cols:]
        return carry

    lax.fori_loop(0, rows // tall, settle, 0)

    center, stretch = table[blocks + 1 : blocks + 2, own], table[blocks + 2 : blocks + 3, own]

    def project(i, carry):
        at = pl.ds(pl.multiple_of(i * step, step), step)
        proj[at, :] = (ext[at, :] - center) * stretch
        return carry

    lax.fori_loop(0, frames // step, project, 0)

    def arrive(up):
        def body(s, carry):
            hop(z, s, up).wait_recv()
            at = pl.ds(pl.multiple_of(s * piece, piece), piece)
            more = decode((from_below if up else from_above)[z, at, :])
            inst[at, :] = inst[at, :] + more[0]
            lag[at, :] = lag[at, :] + more[1]
            return carry

        lax.fori_loop(0, PIECES, body, 0)

    @pl.when(z > 0)
    def _():
        arrive(True)

    @pl.when(z < groups - 1)
    def _():
        arrive(False)

    def finish(d, carry):
        for b in range(1, reps):
            core_copy(d, b).wait_send()

        @pl.when(z < d)
        def _():
            for s in range(PIECES):
                hop(d, s, True).wait_send()

        @pl.when(z > d)
        def _():
            for s in range(PIECES):
                hop(d, s, False).wait_send()

        return carry

    lax.fori_loop(0, groups, finish, 0)

    @pl.when(x == 0)
    def _():
        for k in range(feat_groups):
            h_copy(k).wait_send()

    for ch in range(chunks):
        for copy in fronts[ch] + backs[ch]:
            copy.wait_send()
        for p in range(2):
            for k, o in enumerate(x_steps):
                x_copy(ch, p, k, o).wait_send()


def program(coords, pairs, ids, room, groups, feat_groups, reps):
    cols, width = pairs.shape[1], coords.shape[2]
    feats, frames = cols * feat_groups, coords.shape[1] // groups
    chunks = frames // (feat_groups * 128)
    height = -(-groups * -(-width // 128) // 16) * 16
    blocks = groups * reps
    rows = feats // blocks
    vmem = pl.BlockSpec(memory_space=pltpu.VMEM)
    z_count, x_count, core_count = max(groups - 1, 1), max(feat_groups - 1, 1), max(reps - 1, 1)
    others = max(blocks - 1, 1)
    dma = pltpu.SemaphoreType.DMA
    bf16, f32, i32 = jnp.bfloat16, jnp.float32, jnp.int32
    memory = [
        ((frames, feats), f32),
        ((HALO, cols), f32),
        ((chunks, groups, 3, 128, width), bf16),
        ((feat_groups, 2, cols), i32),
        ((height, 128), f32),
        ((room, width), bf16),
        ((chunks, groups, room, 256), bf16),
        ((chunks, groups, room, 128), bf16),
        ((groups * room, feats), bf16),
        ((chunks, groups * room, 256), bf16),
        ((chunks, groups * room, 128), bf16),
        ((64, feats), f32),
        ((frames + HALO, cols), f32),
        ((frames, 8), f32),
        ((3 * frames, feats), bf16),
        ((3 * frames, 2 * cols), bf16),
        ((groups, reps, rows, 2 * cols), f32),
        ((core_count, groups, rows, 2 * cols), f32),
        ((4, max(feats, 2 * cols)), f32),
        ((blocks, 4, max(feats, 2 * cols)), f32),
        ((blocks + 8, feats), f32),
        ((blocks, 2 * cols), f32),
        ((feats, blocks + 8), f32),
        ((8, 2 * cols), f32),
        ((groups, rows, cols), i32),
        ((groups, rows, cols), i32),
        ((groups, rows, cols), i32),
    ]
    signals = [
        (chunks, groups),
        (x_count,),
        (x_count,),
        (chunks, z_count),
        (chunks, z_count),
        (chunks, z_count),
        (chunks, z_count),
        (chunks,),
        (chunks,),
        (chunks, 2, x_count),
        (chunks, 2, x_count),
        (feat_groups,),
        (1,),
        (core_count, groups),
        (core_count, groups),
        (1,),
        (others,),
        (others,),
        (groups, PIECES),
        (groups, PIECES),
        (groups, PIECES),
    ]
    return pl.pallas_call(
        functools.partial(program_kernel, groups, feat_groups, reps, room, chunks),
        out_shape=(
            jax.ShapeDtypeStruct((rows, cols), f32),
            jax.ShapeDtypeStruct((rows, cols), f32),
            jax.ShapeDtypeStruct((frames, cols), f32),
            jax.ShapeDtypeStruct((1, 1), f32),
        ),
        in_specs=[pl.BlockSpec(memory_space=pl.ANY), vmem, vmem],
        out_specs=(vmem, vmem, vmem, pl.BlockSpec(memory_space=pltpu.SMEM)),
        scratch_shapes=[pltpu.VMEM(*m) for m in memory] + [dma(m) for m in signals],
        compiler_params=pltpu.CompilerParams(
            collective_id=0, has_side_effects=True, vmem_limit_bytes=60 * 1024 * 1024
        ),
    )(coords, pairs, ids)


def encode(inst, lag):
    def one(v):
        root = v * lax.rsqrt(jnp.abs(v) + 1e-30)
        return jnp.round(root * CODE).astype(jnp.int32)

    return (one(inst) << 16) | (one(lag) & 0xFFFF)


def decode(word):
    def one(q):
        root = q.astype(jnp.float32) * (1.0 / CODE)
        return root * jnp.abs(root)

    return one(word >> 16), one((word << 16) >> 16)


def split(value):
    high = value.astype(jnp.bfloat16)
    return high, (value - high.astype(jnp.float32)).astype(jnp.bfloat16)


def write_kernel(*refs):
    count = len(refs) // 2
    ins, outs, sem = refs[:count], refs[count:-1], refs[-1]
    copies = [pltpu.make_async_copy(a, b, sem.at[i]) for i, (a, b) in enumerate(zip(ins, outs))]
    for copy in copies:
        copy.start()
    for copy in copies:
        copy.wait()


def write_out(*arrays):
    vmem, anywhere = pl.BlockSpec(memory_space=pltpu.VMEM), pl.BlockSpec(memory_space=pl.ANY)
    return pl.pallas_call(
        write_kernel,
        out_shape=tuple(jax.ShapeDtypeStruct(a.shape, a.dtype) for a in arrays),
        in_specs=[vmem] * len(arrays),
        out_specs=(anywhere,) * len(arrays),
        scratch_shapes=[pltpu.SemaphoreType.DMA((len(arrays),))],
    )(*arrays)


def slots_per_pass(width, refs, atoms):
    share = width * (1.0 - math.exp(-refs / atoms)) + 1.5 * math.sqrt(width)
    return min(-(-width // 16) * 16, -(-int(share) // 16) * 16)


def collect(value, axis):
    size = lax.axis_size(axis)
    return lax.all_to_all(jnp.broadcast_to(value[None], (size,) + value.shape), axis, 0, 0, tiled=True)


def plain(coords, atom_pairs, traj_ids):
    groups, feat_groups, reps = lax.axis_size("atoms"), lax.axis_size("feat"), lax.axis_size("rep")
    z, x = lax.axis_index("atoms"), lax.axis_index("feat")
    width, cols = coords.shape[2], atom_pairs.shape[1]
    frames = coords.shape[1] // groups
    feats = cols * feat_groups
    exact = lax.Precision.HIGHEST

    split_up = jnp.transpose(coords.reshape(3, groups, frames, width), (1, 0, 2, 3))
    got = lax.all_to_all(split_up, "atoms", 0, 0, tiled=True)
    number = jnp.arange(groups * width, dtype=jnp.int32)[:, None]
    sign = (number == atom_pairs[0]).astype(jnp.bfloat16) - (number == atom_pairs[1]).astype(jnp.bfloat16)
    delta = matmul(got, sign.reshape(groups, width, cols), ((0, 3), (0, 1)))
    own = jnp.sqrt(jnp.sum(delta * delta, 0) + 0.01)
    every = jnp.transpose(collect(own, "feat"), (1, 0, 2)).reshape(frames, feats)
    incoming = lax.ppermute(own[:LAG], "atoms", [(i, (i - 1) % groups) for i in range(groups)])
    future = jnp.concatenate([own[LAG:], incoming], 0)
    ids = jnp.concatenate([traj_ids[0], jnp.full((LAG,), -1, jnp.int32)])
    now = lax.dynamic_slice_in_dim(ids, z * frames, frames)
    later = lax.dynamic_slice_in_dim(ids, z * frames + LAG, frames)
    valid = (now == later).astype(jnp.float32)[:, None]

    def total(value):
        return jnp.sum(collect(jnp.sum(collect(value, "rep"), 0), "atoms"), 0)

    count = total(jnp.full((128,), jnp.sum(valid)))[0]
    mean_now = total(jnp.sum(valid * every, 0)) / count
    mean_next = total(jnp.sum(valid * future, 0)) / count
    now_c, next_c = valid * (every - mean_now), valid * (future - mean_next)
    scale_now = 1.0 / jnp.sqrt(total(jnp.sum(now_c * now_c, 0)) / count + 1e-05)
    scale_next = 1.0 / jnp.sqrt(total(jnp.sum(next_c * next_c, 0)) / count + 1e-05)
    own_c = lax.dynamic_slice_in_dim(now_c, x * cols, cols, 1)
    own_scale = lax.dynamic_slice_in_dim(scale_now, x * cols, cols)
    own_mean = lax.dynamic_slice_in_dim(mean_now, x * cols, cols)
    local = matmul(now_c, jnp.concatenate([own_c, next_c], 1), ((0,), (0,)), exact)
    rows = feats // (groups * reps)
    local = local.reshape(groups, reps, rows, 2 * cols)
    local = jnp.sum(lax.all_to_all(local, "atoms", 0, 0, tiled=True), 0)
    mine = jnp.sum(lax.all_to_all(local, "rep", 0, 0, tiled=True), 0)
    row = (z * reps + lax.axis_index("rep")) * rows
    scale_rows = lax.dynamic_slice_in_dim(scale_now, row, rows)[:, None]
    corr_inst = mine[:, :cols] / count * scale_rows * own_scale
    corr_lag = mine[:, cols:] / count * scale_rows * scale_next
    return corr_inst, corr_lag, (own - own_mean) * own_scale


def shards(atom_coords, atom_pairs, traj_ids):
    groups, feat_groups, reps = lax.axis_size("atoms"), lax.axis_size("feat"), lax.axis_size("rep")
    width = atom_coords.shape[3]
    room = slots_per_pass(width, 2 * atom_pairs.shape[1] * feat_groups, width * groups)
    coords = jnp.transpose(atom_coords[0], (1, 0, 2))
    *results, over = program(coords, atom_pairs, traj_ids, room, groups, feat_groups, reps)
    corr_inst, corr_lag, projections = lax.cond(
        over[0, 0] > room,
        lambda a: plain(coords, atom_pairs, traj_ids),
        lambda a: write_out(*a),
        results,
    )
    return (corr_inst, corr_lag, projections[None])


def solution(mesh):
    placed = (P(("grp", "rep"), None, None, "atoms"), P(None, "feat"), P(("grp", "rep"), None))
    return jax.shard_map(
        shards,
        mesh=mesh,
        in_specs=placed,
        out_specs=(
            P(("grp", "atoms", "rep"), "feat"),
            P(("grp", "atoms", "rep"), "feat"),
            P(("grp", "rep"), "atoms", "feat"),
        ),
        check_vma=False,
    )
```

```python
import functools
import math

import jax
import jax.numpy as jnp
from jax import lax
from jax.experimental import pallas as pl
from jax.experimental.pallas import tpu as pltpu
from jax.sharding import PartitionSpec as P

LAG = 10
HALO = 16
CODE = 32700.0
PIECES = 2


def matmul(left, right, dims, precision=None):
    return lax.dot_general(
        left, right, (dims, ((), ())), precision=precision, preferred_element_type=jnp.float32
    )

MESH = pl.DeviceIdType.MESH


def program_kernel(groups, feat_groups, reps, room, chunks, coords, pairs, ids, inst, lag, proj, over, *scratch):
    (
        every, halo, blocks_in, everyone, ranks, pick, front, back, sign, front_in, back_in, third,
        ext, vcol, left3, right3, local, core, stats, gathered, table, side, columns, scales,
        sums, from_below, from_above,
        load, p_send, p_recv, f_send, f_recv, b_send, b_recv, f_own, b_own, x_send, x_recv, h_send, h_recv,
        c_send, c_recv, s_own, s_send, s_recv, z_send, l_recv, r_recv,
    ) = scratch
    z, r, x = lax.axis_index("atoms"), lax.axis_index("rep"), lax.axis_index("feat")
    peers = [(a, b) for a in range(groups) for b in range(reps) if (a, b) != (0, 0)]
    lanes, part = 128, 64
    width = coords.shape[2]
    feats, cols = every.shape[1], pairs.shape[1]
    half = groups // 2
    z_steps = [half] + [o for o in range(groups - 1, 0, -1) if o != half] if groups > 1 else []
    x_steps = list(range(1, feat_groups))
    frames_here = feat_groups * chunks * lanes
    z_dests = [lax.rem(z + o, groups) for o in z_steps] + [z]
    loads = []
    for ch in range(chunks):
        row = []
        for i, dest in enumerate(z_dests):
            start = pl.multiple_of(dest * frames_here + (x * chunks + ch) * lanes, 16)
            row.append(
                pltpu.make_async_copy(coords.at[:, pl.ds(start, lanes), :], blocks_in.at[ch, i], load.at[ch, i])
            )
            row[-1].start()
        loads.append(row)
    barrier = pltpu.get_barrier_semaphore()

    def peer(a, b):
        return {"atoms": lax.rem(z + a, groups), "rep": lax.rem(r + b, reps)}

    for a, b in peers:
        pl.semaphore_signal(barrier, 1, device_id=peer(a, b), device_id_type=MESH)
    for o in x_steps:
        pl.semaphore_signal(barrier, 1, device_id={"feat": lax.rem(x + o, feat_groups)}, device_id_type=MESH)
    z_up, z_down = lax.rem(z + 1, groups), lax.rem(z + groups - 1, groups)

    @pl.when(x == 0)
    def _():
        for k in x_steps:
            pl.semaphore_signal(barrier, 1, device_id={"atoms": z_down, "feat": k}, device_id_type=MESH)

    @pl.when(x != 0)
    def _():
        pl.semaphore_signal(barrier, 1, device_id={"atoms": z_up, "feat": 0}, device_id_type=MESH)

    everyone[x] = pairs[...]

    @pl.when(x == 0)
    def _():
        pl.semaphore_wait(barrier, len(peers) + 2 * len(x_steps))

    @pl.when(x != 0)
    def _():
        pl.semaphore_wait(barrier, len(peers) + len(x_steps) + 1)

    pair_copies = []
    for k, o in enumerate(x_steps):
        pair_copies.append(
            pltpu.make_async_remote_copy(
                src_ref=pairs,
                dst_ref=everyone.at[x],
                send_sem=p_send.at[k],
                recv_sem=p_recv.at[k],
                device_id={"feat": lax.rem(x + o, feat_groups)},
                device_id_type=MESH,
            )
        )
        pair_copies[-1].start()
    for copy in pair_copies:
        copy.wait()

    lines = -(-width // lanes)
    height = -(-groups * lines // 16) * 16

    def iota(shape, dim):
        return lax.broadcasted_iota(jnp.int32, shape, dim)

    def bins(value, size):
        return sum(((value >= s * size).astype(jnp.int32) for s in range(1, groups)), jnp.zeros_like(value))

    def ones(mask):
        return jnp.where(mask, 1.0, 0.0).astype(jnp.bfloat16)

    def product(a, b, dims):
        return lax.dot_general(a, b, (dims, ((), ())), preferred_element_type=jnp.float32)

    found, counts = [], jnp.zeros((height, lanes), jnp.float32)
    for k in range(2):
        ref = jnp.concatenate([everyone[i, k : k + 1, :] for i in range(feat_groups)], 1)
        shard = bins(ref, width)
        inner = ref - shard * width
        line = ones(iota((height, feats), 0) == shard * lines + (inner >> 7))
        spot = ones(iota((lanes, feats), 0) == (inner & 127))
        counts = counts + product(line, spot, ((1,), (1,)))
        found.append((shard, line, spot))
    used = ones(counts > 0.5)
    earlier = ones(iota((lanes, lanes), 0) < iota((lanes, lanes), 1))
    row_shard, col_shard = bins(iota((height, height), 0), lines), bins(iota((height, height), 1), lines)
    same = row_shard == col_shard
    filled = product(used, jnp.ones((lanes, lanes), jnp.bfloat16), ((1,), (0,))).astype(jnp.bfloat16)
    before = product(
        ones(same & (iota((height, height), 1) < iota((height, height), 0))), filled, ((1,), (0,))
    )
    rank = product(used, earlier, ((1,), (0,))) + before
    most = jnp.max(product(ones(same), filled, ((1,), (0,))))
    over[0, 0] = most
    ranks[...] = jnp.where(counts > 0.5, rank, -1.0)
    whole = rank.astype(jnp.int32)
    parts = jnp.concatenate(
        [(whole >> 4).astype(jnp.float32), (whole & 15).astype(jnp.float32)], 0
    ).astype(jnp.bfloat16)
    slots = []
    for shard, line, spot in found:
        got = product(parts, spot, ((1,), (0,)))
        chosen = (got[:height] * 16.0 + got[height:]) * line.astype(jnp.float32)
        place = jnp.sum(chosen, 0, keepdims=True).astype(jnp.int32)
        slots.append(jnp.where(place < room, shard * room + place, -1))

    slot_no = iota((room, lanes), 0).astype(jnp.float32)
    for j in range(lines):
        wide = min(lanes, width - j * lanes)
        row = ranks[pl.ds(z * lines + j, 1), :]
        pick[:, j * lanes : j * lanes + wide] = ones(slot_no == row)[:, :wide]

    def fill(ch, i):
        loads[ch][i].wait()

        def get(first):
            return product(pick[...], first, ((1,), (1,))).astype(jnp.bfloat16)

        early = [blocks_in[ch, i, c, :part] for c in range(2)]
        late = [blocks_in[ch, i, c, part:] for c in range(2)]
        front[ch, i, :, :lanes] = get(jnp.concatenate(early, 0))
        front[ch, i, :, lanes:] = get(blocks_in[ch, i, 2])
        back[ch, i] = get(jnp.concatenate(late, 0))

    here = pl.ds(pl.multiple_of(z * room, 16), room)

    def z_copy(source, target, send, recv, ch, i):
        return pltpu.make_async_remote_copy(
            src_ref=source.at[ch, i],
            dst_ref=target.at[ch, here],
            send_sem=send.at[ch, i],
            recv_sem=recv.at[ch, i],
            device_id={"atoms": z_dests[i]},
            device_id_type=MESH,
        )

    fronts, backs = [], []
    for ch in range(chunks):
        fronts.append([])
        backs.append([])
        for i in range(len(z_steps)):
            fill(ch, i)
            fronts[ch].append(z_copy(front, front_in, f_send, f_recv, ch, i))
            fronts[ch][i].start()
        for i in range(len(z_steps)):
            backs[ch].append(z_copy(back, back_in, b_send, b_recv, ch, i))
            backs[ch][i].start()
    last = len(z_steps)
    front_own, back_own = [], []
    for ch in range(chunks):
        fill(ch, last)
        front_own.append(pltpu.make_async_copy(front.at[ch, last], front_in.at[ch, here], f_own.at[ch]))
        back_own.append(pltpu.make_async_copy(back.at[ch, last], back_in.at[ch, here], b_own.at[ch]))
        front_own[ch].start()
        back_own[ch].start()

    def make_sign(i, carry):
        at = pl.ds(pl.multiple_of(i * 16, 16), 16)
        number = iota((16, feats), 0) + i * 16
        value = jnp.where(number == slots[0], 1.0, 0.0) - jnp.where(number == slots[1], 1.0, 0.0)
        sign[at, :] = value.astype(jnp.bfloat16)
        return carry

    lax.fori_loop(0, groups * room // 16, make_sign, 0)

    def x_copy(ch, p, k, o):
        at = every.at[pl.ds(pl.multiple_of((x * chunks + ch) * lanes + p * part, part), part), :]
        return pltpu.make_async_remote_copy(
            src_ref=at,
            dst_ref=at,
            send_sem=x_send.at[ch, p, k],
            recv_sem=x_recv.at[ch, p, k],
            device_id={"feat": lax.rem(x + o, feat_groups)},
            device_id_type=MESH,
        )

    def h_copy(k):
        return pltpu.make_async_remote_copy(
            src_ref=every.at[:HALO, k * cols : (k + 1) * cols],
            dst_ref=halo,
            send_sem=h_send.at[k],
            recv_sem=h_recv.at[0],
            device_id={"atoms": z_down, "feat": k},
            device_id_type=MESH,
        )

    def keep(ch, p, total):
        at = pl.ds(pl.multiple_of((x * chunks + ch) * lanes + p * part, part), part)
        every[at, :] = jnp.sqrt(total + 0.01)
        for k, o in enumerate(x_steps):
            x_copy(ch, p, k, o).start()

    for ch in range(chunks):
        front_own[ch].wait()
        for copy in fronts[ch]:
            copy.wait_recv()
        delta = product(front_in[ch], sign[...], ((0,), (0,)))
        square = delta * delta
        third[...] = square[3 * part :]
        keep(ch, 0, square[:part] + square[part : 2 * part] + square[2 * part : 3 * part])
        if ch == 0:

            @pl.when(x == 0)
            def _():
                for k in range(feat_groups):
                    h_copy(k).start()

        back_own[ch].wait()
        for copy in backs[ch]:
            copy.wait_recv()
        delta = product(back_in[ch], sign[...], ((0,), (0,)))
        square = delta * delta
        keep(ch, 1, square[:part] + square[part:] + third[...])

    h_copy(0).wait_recv()
    for ch in range(chunks):
        for p in range(2):
            for k, o in enumerate(x_steps):
                x_copy(ch, p, k, o).wait_recv()

    frames, rows, blocks = frames_here, inst.shape[0], groups * reps
    me = z * reps + r
    present = ids[:, pl.ds(pl.multiple_of(z * frames, 128), frames)]
    after = ids[:, pl.ds(pl.multiple_of(jnp.minimum(z + 1, groups - 1) * frames, 128), 128)]
    after = jnp.where(z == groups - 1, -1, after)
    names = jnp.concatenate([present, after], 1).astype(jnp.float32)
    names = jnp.broadcast_to(names, (8, frames + 128))
    later = pltpu.roll(names, frames + 128 - LAG, 1)
    valid = (names == later).astype(jnp.float32)[:, :frames]
    count = jnp.sum(valid[:1], axis=1, keepdims=True)
    inverse = 1.0 / jnp.maximum(count, 1.0)
    vcol[...] = valid.T

    own = pl.ds(pl.multiple_of(x * cols, 128), cols)
    ext[:frames, :] = every[:, own]
    ext[frames:, :] = halo[...]
    step = 32

    def moved(i):
        wide = ext[pl.ds(pl.multiple_of(i * step, step), step + 16), :]
        return pltpu.roll(wide, step + 16 - LAG, 0)[:step]

    def fold(value):
        return jnp.sum(value.reshape(step // 8, 8, value.shape[1]), 0)

    def first(i, carry):
        at = pl.ds(pl.multiple_of(i * step, step), step)
        weight = vcol[at, :1]
        return carry[0] + fold(every[at, :] * weight), carry[1] + fold(moved(i) * weight)

    zero = (jnp.zeros((8, feats), jnp.float32), jnp.zeros((8, cols), jnp.float32))
    now_sum, next_sum = lax.fori_loop(0, frames // step, first, zero)
    now_mean = jnp.sum(now_sum, 0, keepdims=True) * inverse
    next_mean = jnp.sum(next_sum, 0, keepdims=True) * inverse

    def second(i, carry):
        base = pl.multiple_of(i * step, step)
        at, at1, at2 = pl.ds(base, step), pl.ds(base + frames, step), pl.ds(base + 2 * frames, step)
        weight = vcol[at, :1]
        now = (every[at, :] - now_mean) * weight
        later = (moved(i) - next_mean) * weight
        high, low = split(now)
        left3[at, :] = high
        left3[at1, :] = high
        left3[at2, :] = low
        right3[at, :cols] = left3[at, own]
        right3[at1, :cols] = left3[at2, own]
        right3[at2, :cols] = left3[at, own]
        high, low = split(later)
        right3[at, cols:] = high
        right3[at1, cols:] = low
        right3[at2, cols:] = high
        return carry[0] + fold(now * now), carry[1] + fold(later * later)

    now_sq, next_sq = lax.fori_loop(0, frames // step, second, zero)
    stats[0:1, :] = now_mean
    stats[1:2, :] = jnp.sum(now_sq, 0, keepdims=True)
    stats[2:3, :cols] = next_mean
    stats[2:3, cols : 2 * cols] = jnp.sum(next_sq, 0, keepdims=True)
    stats[3:4, :feats] = jnp.broadcast_to(count, (1, feats))

    own_stats = pltpu.make_async_copy(stats, gathered.at[me], s_own.at[0])
    own_stats.start()
    stat_copies = []
    for k, (a, b) in enumerate(peers):
        stat_copies.append(
            pltpu.make_async_remote_copy(
                src_ref=stats,
                dst_ref=gathered.at[me],
                send_sem=s_send.at[k],
                recv_sem=s_recv.at[k],
                device_id=peer(a, b),
                device_id_type=MESH,
            )
        )
        stat_copies[-1].start()

    def core_copy(d, b):
        return pltpu.make_async_remote_copy(
            src_ref=local.at[d, lax.rem(r + b, reps)],
            dst_ref=core.at[b - 1, d],
            send_sem=c_send.at[b - 1, d],
            recv_sem=c_recv.at[b - 1, d],
            device_id={"rep": lax.rem(r + b, reps)},
            device_id_type=MESH,
        )

    tile = max(128, reps * rows)
    tiles, inside = feats // tile, tile // (reps * rows)

    def multiply(k, carry):
        half = k // 2
        t = jnp.where(k % 2 == 0, tiles - 1 - half, half)
        at = pl.ds(pl.multiple_of(t * tile, tile), tile)
        got = lax.dot_general(
            left3[:, at], right3[...], (((0,), (0,)), ((), ())), preferred_element_type=jnp.float32
        )
        for j in range(inside):
            d = t * inside + j
            for b in range(reps):
                low = (j * reps + b) * rows
                local[d, b] = got[low : low + rows]
            for b in range(1, reps):
                core_copy(d, b).start()
        return carry

    lax.fori_loop(0, tiles, multiply, 0)

    own_stats.wait()
    for copy in stat_copies:
        copy.wait()

    total = jnp.zeros((1, feats), jnp.float32)
    now_total = jnp.zeros((1, feats), jnp.float32)
    next_total = jnp.zeros((1, cols), jnp.float32)
    for b in range(blocks):
        size = gathered[b, 3:4, :feats]
        total = total + size
        now_total = now_total + size * gathered[b, 0:1, :feats]
        next_total = next_total + size[:, :cols] * gathered[b, 2:3, :cols]
    mean_now = now_total / total
    mean_next = next_total / total[:, :cols]
    now_spread = jnp.zeros((1, feats), jnp.float32)
    next_spread = jnp.zeros((1, cols), jnp.float32)
    for b in range(blocks):
        size = gathered[b, 3:4, :feats]
        off = gathered[b, 0:1, :feats] - mean_now
        now_spread = now_spread + (gathered[b, 1:2, :feats] + size * off * off)
        off = gathered[b, 2:3, :cols] - mean_next
        next_spread = next_spread + (gathered[b, 2:3, cols : 2 * cols] + size[:, :cols] * off * off)
    scale_now = 1.0 / jnp.sqrt(now_spread / total + 1e-05)
    scale_next = 1.0 / jnp.sqrt(next_spread / total[:, :cols] + 1e-05)
    root = 1.0 / jnp.sqrt(total)
    table[blocks : blocks + 1, :] = scale_now * root
    table[blocks + 1 : blocks + 2, :] = mean_now
    table[blocks + 2 : blocks + 3, :] = scale_now
    table[blocks + 3 :, :] = jnp.zeros((5, feats), jnp.float32)
    for b in range(blocks):
        size = gathered[b, 3:4, :feats]
        table[b : b + 1, :] = (gathered[b, 0:1, :feats] - mean_now) * (scale_now * root)
        side[b : b + 1, cols:] = (
            size[:, :cols] * (gathered[b, 2:3, :cols] - mean_next) * (scale_next * root[:, :cols])
        )
    for b in range(blocks):
        side[b : b + 1, :cols] = gathered[b, 3:4, :cols] * table[b : b + 1, own]
    scales[0:1, :cols] = table[blocks : blocks + 1, own]
    scales[0:1, cols:] = scale_next * root[:, :cols]
    columns[...] = table[...].T

    tall = min(rows // PIECES, 32)
    piece = rows // PIECES

    def hop(d, s, up):
        at = pl.ds(pl.multiple_of(s * piece, piece), piece)
        return pltpu.make_async_remote_copy(
            src_ref=sums.at[d, at],
            dst_ref=(from_below if up else from_above).at[d, at],
            send_sem=z_send.at[d, s],
            recv_sem=(l_recv if up else r_recv).at[d, s],
            device_id={"atoms": lax.rem(z + (1 if up else groups - 1), groups)},
            device_id_type=MESH,
        )

    def mine(d, i):
        at = pl.ds(pl.multiple_of(i * tall, tall), tall)
        value = local[d, r, at, :]
        for b in range(1, reps):
            value = value + core[b - 1, d, at, :]
        high = pl.ds(pl.multiple_of((d * reps + r) * rows + i * tall, tall), tall)
        return value * columns[high, blocks : blocks + 1] * scales[0:1, :]

    def wait_core(d):
        for b in range(1, reps):
            core_copy(d, b).wait_recv()

    def send(d, s, up, relay):
        if relay:
            hop(d, s, up).wait_recv()

        def body(j, carry):
            i = s * (piece // tall) + j
            at = pl.ds(pl.multiple_of(i * tall, tall), tall)
            value = mine(d, i)
            inst_part, lag_part = value[:, :cols], value[:, cols:]
            if relay:
                more = decode((from_below if up else from_above)[d, at, :])
                inst_part, lag_part = inst_part + more[0], lag_part + more[1]
            sums[d, at, :] = encode(inst_part, lag_part)
            return carry

        lax.fori_loop(0, piece // tall, body, 0)
        hop(d, s, up).start()

    turn_above = PIECES * z
    turn_below = PIECES * (groups - 1 - z) + jnp.where(z >= groups // 2, 1, 0)

    def chain(turn, carry):
        down, up = turn - turn_below, turn - turn_above

        @pl.when((down >= 0) & (down < PIECES * z))
        def _():
            below, s = down // PIECES, down % PIECES

            @pl.when(s == 0)
            def _():
                wait_core(below)

            @pl.when(z == groups - 1)
            def _():
                send(below, s, False, False)

            @pl.when(z < groups - 1)
            def _():
                send(below, s, False, True)

        @pl.when((up >= 0) & (up < PIECES * (groups - 1 - z)))
        def _():
            above, s = groups - 1 - up // PIECES, up % PIECES

            @pl.when(s == 0)
            def _():
                wait_core(above)

            @pl.when(z == 0)
            def _():
                send(above, s, True, False)

            @pl.when(z > 0)
            def _():
                send(above, s, True, True)

        return carry

    lax.fori_loop(0, PIECES * (groups - 1) + 1, chain, 0)

    wait_core(z)

    def settle(i, carry):
        at = pl.ds(pl.multiple_of(i * tall, tall), tall)
        high = pl.ds(pl.multiple_of(me * rows + i * tall, tall), tall)
        shift = lax.dot_general(
            columns[high, :blocks], side[...], (((1,), (0,)), ((), ())),
            precision=lax.Precision.HIGHEST, preferred_element_type=jnp.float32,
        )
        value = mine(z, i) + shift
        inst[at, :] = value[:, :cols]
        lag[at, :] = value[:, cols:]
        return carry

    lax.fori_loop(0, rows // tall, settle, 0)

    center, stretch = table[blocks + 1 : blocks + 2, own], table[blocks + 2 : blocks + 3, own]

    def project(i, carry):
        at = pl.ds(pl.multiple_of(i * step, step), step)
        proj[at, :] = (ext[at, :] - center) * stretch
        return carry

    lax.fori_loop(0, frames // step, project, 0)

    def arrive(up):
        def body(s, carry):
            hop(z, s, up).wait_recv()
            at = pl.ds(pl.multiple_of(s * piece, piece), piece)
            more = decode((from_below if up else from_above)[z, at, :])
            inst[at, :] = inst[at, :] + more[0]
            lag[at, :] = lag[at, :] + more[1]
            return carry

        lax.fori_loop(0, PIECES, body, 0)

    @pl.when(z > 0)
    def _():
        arrive(True)

    @pl.when(z < groups - 1)
    def _():
        arrive(False)

    def finish(d, carry):
        for b in range(1, reps):
            core_copy(d, b).wait_send()

        @pl.when(z < d)
        def _():
            for s in range(PIECES):
                hop(d, s, True).wait_send()

        @pl.when(z > d)
        def _():
            for s in range(PIECES):
                hop(d, s, False).wait_send()

        return carry

    lax.fori_loop(0, groups, finish, 0)

    @pl.when(x == 0)
    def _():
        for k in range(feat_groups):
            h_copy(k).wait_send()

    for ch in range(chunks):
        for copy in fronts[ch] + backs[ch]:
            copy.wait_send()
        for p in range(2):
            for k, o in enumerate(x_steps):
                x_copy(ch, p, k, o).wait_send()


def program(coords, pairs, ids, room, groups, feat_groups, reps):
    cols, width = pairs.shape[1], coords.shape[2]
    feats, frames = cols * feat_groups, coords.shape[1] // groups
    chunks = frames // (feat_groups * 128)
    height = -(-groups * -(-width // 128) // 16) * 16
    blocks = groups * reps
    rows = feats // blocks
    vmem = pl.BlockSpec(memory_space=pltpu.VMEM)
    z_count, x_count, core_count = max(groups - 1, 1), max(feat_groups - 1, 1), max(reps - 1, 1)
    others = max(blocks - 1, 1)
    dma = pltpu.SemaphoreType.DMA
    bf16, f32, i32 = jnp.bfloat16, jnp.float32, jnp.int32
    memory = [
        ((frames, feats), f32),
        ((HALO, cols), f32),
        ((chunks, groups, 3, 128, width), bf16),
        ((feat_groups, 2, cols), i32),
        ((height, 128), f32),
        ((room, width), bf16),
        ((chunks, groups, room, 256), bf16),
        ((chunks, groups, room, 128), bf16),
        ((groups * room, feats), bf16),
        ((chunks, groups * room, 256), bf16),
        ((chunks, groups * room, 128), bf16),
        ((64, feats), f32),
        ((frames + HALO, cols), f32),
        ((frames, 8), f32),
        ((3 * frames, feats), bf16),
        ((3 * frames, 2 * cols), bf16),
        ((groups, reps, rows, 2 * cols), f32),
        ((core_count, groups, rows, 2 * cols), f32),
        ((4, max(feats, 2 * cols)), f32),
        ((blocks, 4, max(feats, 2 * cols)), f32),
        ((blocks + 8, feats), f32),
        ((blocks, 2 * cols), f32),
        ((feats, blocks + 8), f32),
        ((8, 2 * cols), f32),
        ((groups, rows, cols), i32),
        ((groups, rows, cols), i32),
        ((groups, rows, cols), i32),
    ]
    signals = [
        (chunks, groups),
        (x_count,),
        (x_count,),
        (chunks, z_count),
        (chunks, z_count),
        (chunks, z_count),
        (chunks, z_count),
        (chunks,),
        (chunks,),
        (chunks, 2, x_count),
        (chunks, 2, x_count),
        (feat_groups,),
        (1,),
        (core_count, groups),
        (core_count, groups),
        (1,),
        (others,),
        (others,),
        (groups, PIECES),
        (groups, PIECES),
        (groups, PIECES),
    ]
    return pl.pallas_call(
        functools.partial(program_kernel, groups, feat_groups, reps, room, chunks),
        out_shape=(
            jax.ShapeDtypeStruct((rows, cols), f32),
            jax.ShapeDtypeStruct((rows, cols), f32),
            jax.ShapeDtypeStruct((frames, cols), f32),
            jax.ShapeDtypeStruct((1, 1), f32),
        ),
        in_specs=[pl.BlockSpec(memory_space=pl.ANY), vmem, vmem],
        out_specs=(vmem, vmem, vmem, pl.BlockSpec(memory_space=pltpu.SMEM)),
        scratch_shapes=[pltpu.VMEM(*m) for m in memory] + [dma(m) for m in signals],
        compiler_params=pltpu.CompilerParams(
            collective_id=0, has_side_effects=True, vmem_limit_bytes=60 * 1024 * 1024
        ),
    )(coords, pairs, ids)


def encode(inst, lag):
    def one(v):
        root = v * lax.rsqrt(jnp.abs(v) + 1e-30)
        return jnp.round(root * CODE).astype(jnp.int32)

    return (one(inst) << 16) | (one(lag) & 0xFFFF)


def decode(word):
    def one(q):
        root = q.astype(jnp.float32) * (1.0 / CODE)
        return root * jnp.abs(root)

    return one(word >> 16), one((word << 16) >> 16)


def split(value):
    high = value.astype(jnp.bfloat16)
    return high, (value - high.astype(jnp.float32)).astype(jnp.bfloat16)


def write_kernel(*refs):
    count = len(refs) // 2
    ins, outs, sem = refs[:count], refs[count:-1], refs[-1]
    copies = [pltpu.make_async_copy(a, b, sem.at[i]) for i, (a, b) in enumerate(zip(ins, outs))]
    for copy in copies:
        copy.start()
    for copy in copies:
        copy.wait()


def write_out(*arrays):
    vmem, anywhere = pl.BlockSpec(memory_space=pltpu.VMEM), pl.BlockSpec(memory_space=pl.ANY)
    return pl.pallas_call(
        write_kernel,
        out_shape=tuple(jax.ShapeDtypeStruct(a.shape, a.dtype) for a in arrays),
        in_specs=[vmem] * len(arrays),
        out_specs=(anywhere,) * len(arrays),
        scratch_shapes=[pltpu.SemaphoreType.DMA((len(arrays),))],
    )(*arrays)


def slots_per_pass(width, refs, atoms):
    share = width * (1.0 - math.exp(-refs / atoms)) + 1.5 * math.sqrt(width)
    return min(-(-width // 16) * 16, -(-int(share) // 16) * 16)


def collect(value, axis):
    size = lax.axis_size(axis)
    return lax.all_to_all(jnp.broadcast_to(value[None], (size,) + value.shape), axis, 0, 0, tiled=True)


def plain(coords, atom_pairs, traj_ids):
    groups, feat_groups, reps = lax.axis_size("atoms"), lax.axis_size("feat"), lax.axis_size("rep")
    z, x = lax.axis_index("atoms"), lax.axis_index("feat")
    width, cols = coords.shape[2], atom_pairs.shape[1]
    frames = coords.shape[1] // groups
    feats = cols * feat_groups
    exact = lax.Precision.HIGHEST

    split_up = jnp.transpose(coords.reshape(3, groups, frames, width), (1, 0, 2, 3))
    got = lax.all_to_all(split_up, "atoms", 0, 0, tiled=True)
    number = jnp.arange(groups * width, dtype=jnp.int32)[:, None]
    sign = (number == atom_pairs[0]).astype(jnp.bfloat16) - (number == atom_pairs[1]).astype(jnp.bfloat16)
    delta = matmul(got, sign.reshape(groups, width, cols), ((0, 3), (0, 1)))
    own = jnp.sqrt(jnp.sum(delta * delta, 0) + 0.01)
    every = jnp.transpose(collect(own, "feat"), (1, 0, 2)).reshape(frames, feats)
    incoming = lax.ppermute(own[:LAG], "atoms", [(i, (i - 1) % groups) for i in range(groups)])
    future = jnp.concatenate([own[LAG:], incoming], 0)
    ids = jnp.concatenate([traj_ids[0], jnp.full((LAG,), -1, jnp.int32)])
    now = lax.dynamic_slice_in_dim(ids, z * frames, frames)
    later = lax.dynamic_slice_in_dim(ids, z * frames + LAG, frames)
    valid = (now == later).astype(jnp.float32)[:, None]

    def total(value):
        return jnp.sum(collect(jnp.sum(collect(value, "rep"), 0), "atoms"), 0)

    count = total(jnp.full((128,), jnp.sum(valid)))[0]
    mean_now = total(jnp.sum(valid * every, 0)) / count
    mean_next = total(jnp.sum(valid * future, 0)) / count
    now_c, next_c = valid * (every - mean_now), valid * (future - mean_next)
    scale_now = 1.0 / jnp.sqrt(total(jnp.sum(now_c * now_c, 0)) / count + 1e-05)
    scale_next = 1.0 / jnp.sqrt(total(jnp.sum(next_c * next_c, 0)) / count + 1e-05)
    own_c = lax.dynamic_slice_in_dim(now_c, x * cols, cols, 1)
    own_scale = lax.dynamic_slice_in_dim(scale_now, x * cols, cols)
    own_mean = lax.dynamic_slice_in_dim(mean_now, x * cols, cols)
    local = matmul(now_c, jnp.concatenate([own_c, next_c], 1), ((0,), (0,)), exact)
    rows = feats // (groups * reps)
    local = local.reshape(groups, reps, rows, 2 * cols)
    local = jnp.sum(lax.all_to_all(local, "atoms", 0, 0, tiled=True), 0)
    mine = jnp.sum(lax.all_to_all(local, "rep", 0, 0, tiled=True), 0)
    row = (z * reps + lax.axis_index("rep")) * rows
    scale_rows = lax.dynamic_slice_in_dim(scale_now, row, rows)[:, None]
    corr_inst = mine[:, :cols] / count * scale_rows * own_scale
    corr_lag = mine[:, cols:] / count * scale_rows * scale_next
    return corr_inst, corr_lag, (own - own_mean) * own_scale


def shards(atom_coords, atom_pairs, traj_ids):
    groups, feat_groups, reps = lax.axis_size("atoms"), lax.axis_size("feat"), lax.axis_size("rep")
    width = atom_coords.shape[3]
    room = slots_per_pass(width, 2 * atom_pairs.shape[1] * feat_groups, width * groups)
    coords = jnp.transpose(atom_coords[0], (1, 0, 2))
    *results, over = program(coords, atom_pairs, traj_ids, room, groups, feat_groups, reps)
    corr_inst, corr_lag, projections = lax.cond(
        over[0, 0] > room,
        lambda a: plain(coords, atom_pairs, traj_ids),
        lambda a: write_out(*a),
        results,
    )
    return (corr_inst, corr_lag, projections[None])


def solution(mesh):
    placed = (P(("grp", "rep"), None, None, "atoms"), P(None, "feat"), P(("grp", "rep"), None))
    return jax.shard_map(
        shards,
        mesh=mesh,
        in_specs=placed,
        out_specs=(
            P(("grp", "atoms", "rep"), "feat"),
            P(("grp", "atoms", "rep"), "feat"),
            P(("grp", "rep"), "atoms", "feat"),
        ),
        check_vma=False,
    )
```

```python
import functools
import math

import jax
import jax.numpy as jnp
from jax import lax
from jax.experimental import pallas as pl
from jax.experimental.pallas import tpu as pltpu
from jax.sharding import PartitionSpec as P

LAG = 10
HALO = 16
CODE = 32700.0
PIECES = 2


def matmul(left, right, dims, precision=None):
    return lax.dot_general(
        left, right, (dims, ((), ())), precision=precision, preferred_element_type=jnp.float32
    )

MESH = pl.DeviceIdType.MESH


def program_kernel(groups, feat_groups, reps, room, chunks, coords, pairs, ids, inst, lag, proj, over, *scratch):
    (
        every, halo, blocks_in, everyone, ranks, pick, front, back, sign, front_in, back_in, third,
        shift, sums_now, sums_next, vcol, left3, right3, local, core, stats, gathered, table, side, columns, scales,
        sums, from_below, from_above,
        load, p_send, p_recv, f_send, f_recv, b_send, b_recv, f_own, b_own, x_send, x_recv, h_send, h_recv,
        c_send, c_recv, s_own, s_send, s_recv, z_send, l_recv, r_recv,
    ) = scratch
    z, r, x = lax.axis_index("atoms"), lax.axis_index("rep"), lax.axis_index("feat")
    peers = [(a, b) for a in range(groups) for b in range(reps) if (a, b) != (0, 0)]
    lanes, part = 128, 64
    width = coords.shape[2]
    feats, cols = every.shape[1], pairs.shape[1]
    half = groups // 2
    z_steps = [half] + [o for o in range(groups - 1, 0, -1) if o != half] if groups > 1 else []
    x_steps = list(range(1, feat_groups))
    frames_here = feat_groups * chunks * lanes
    z_dests = [lax.rem(z + o, groups) for o in z_steps] + [z]
    loads = []
    for ch in range(chunks):
        row = []
        for i, dest in enumerate(z_dests):
            start = pl.multiple_of(dest * frames_here + (x * chunks + ch) * lanes, 16)
            row.append(
                pltpu.make_async_copy(coords.at[:, pl.ds(start, lanes), :], blocks_in.at[ch, i], load.at[ch, i])
            )
            row[-1].start()
        loads.append(row)
    barrier = pltpu.get_barrier_semaphore()

    def peer(a, b):
        return {"atoms": lax.rem(z + a, groups), "rep": lax.rem(r + b, reps)}

    for a, b in peers:
        pl.semaphore_signal(barrier, 1, device_id=peer(a, b), device_id_type=MESH)
    for o in x_steps:
        pl.semaphore_signal(barrier, 1, device_id={"feat": lax.rem(x + o, feat_groups)}, device_id_type=MESH)
    z_up, z_down = lax.rem(z + 1, groups), lax.rem(z + groups - 1, groups)

    @pl.when(x == 0)
    def _():
        for k in x_steps:
            pl.semaphore_signal(barrier, 1, device_id={"atoms": z_down, "feat": k}, device_id_type=MESH)

    @pl.when(x != 0)
    def _():
        pl.semaphore_signal(barrier, 1, device_id={"atoms": z_up, "feat": 0}, device_id_type=MESH)

    everyone[x] = pairs[...]

    @pl.when(x == 0)
    def _():
        pl.semaphore_wait(barrier, len(peers) + 2 * len(x_steps))

    @pl.when(x != 0)
    def _():
        pl.semaphore_wait(barrier, len(peers) + len(x_steps) + 1)

    pair_copies = []
    for k, o in enumerate(x_steps):
        pair_copies.append(
            pltpu.make_async_remote_copy(
                src_ref=pairs,
                dst_ref=everyone.at[x],
                send_sem=p_send.at[k],
                recv_sem=p_recv.at[k],
                device_id={"feat": lax.rem(x + o, feat_groups)},
                device_id_type=MESH,
            )
        )
        pair_copies[-1].start()
    for copy in pair_copies:
        copy.wait()

    lines = -(-width // lanes)
    height = -(-groups * lines // 16) * 16

    def iota(shape, dim):
        return lax.broadcasted_iota(jnp.int32, shape, dim)

    def bins(value, size):
        return sum(((value >= s * size).astype(jnp.int32) for s in range(1, groups)), jnp.zeros_like(value))

    def ones(mask):
        return jnp.where(mask, 1.0, 0.0).astype(jnp.bfloat16)

    def product(a, b, dims):
        return lax.dot_general(a, b, (dims, ((), ())), preferred_element_type=jnp.float32)

    found, counts = [], jnp.zeros((height, lanes), jnp.float32)
    for k in range(2):
        ref = jnp.concatenate([everyone[i, k : k + 1, :] for i in range(feat_groups)], 1)
        shard = bins(ref, width)
        inner = ref - shard * width
        line = ones(iota((height, feats), 0) == shard * lines + (inner >> 7))
        spot = ones(iota((lanes, feats), 0) == (inner & 127))
        counts = counts + product(line, spot, ((1,), (1,)))
        found.append((shard, line, spot))
    used = ones(counts > 0.5)
    earlier = ones(iota((lanes, lanes), 0) < iota((lanes, lanes), 1))
    row_shard, col_shard = bins(iota((height, height), 0), lines), bins(iota((height, height), 1), lines)
    same = row_shard == col_shard
    filled = product(used, jnp.ones((lanes, lanes), jnp.bfloat16), ((1,), (0,))).astype(jnp.bfloat16)
    before = product(
        ones(same & (iota((height, height), 1) < iota((height, height), 0))), filled, ((1,), (0,))
    )
    rank = product(used, earlier, ((1,), (0,))) + before
    most = jnp.max(product(ones(same), filled, ((1,), (0,))))
    over[0, 0] = most
    ranks[...] = jnp.where(counts > 0.5, rank, -1.0)
    whole = rank.astype(jnp.int32)
    parts = jnp.concatenate(
        [(whole >> 4).astype(jnp.float32), (whole & 15).astype(jnp.float32)], 0
    ).astype(jnp.bfloat16)
    slots = []
    for shard, line, spot in found:
        got = product(parts, spot, ((1,), (0,)))
        chosen = (got[:height] * 16.0 + got[height:]) * line.astype(jnp.float32)
        place = jnp.sum(chosen, 0, keepdims=True).astype(jnp.int32)
        slots.append(jnp.where(place < room, shard * room + place, -1))

    slot_no = iota((room, lanes), 0).astype(jnp.float32)
    for j in range(lines):
        wide = min(lanes, width - j * lanes)
        row = ranks[pl.ds(z * lines + j, 1), :]
        pick[:, j * lanes : j * lanes + wide] = ones(slot_no == row)[:, :wide]

    def fill(ch, i):
        loads[ch][i].wait()

        def get(first):
            return product(pick[...], first, ((1,), (1,))).astype(jnp.bfloat16)

        early = [blocks_in[ch, i, c, :part] for c in range(2)]
        late = [blocks_in[ch, i, c, part:] for c in range(2)]
        front[ch, i, :, :lanes] = get(jnp.concatenate(early, 0))
        front[ch, i, :, lanes:] = get(blocks_in[ch, i, 2])
        back[ch, i] = get(jnp.concatenate(late, 0))

    here = pl.ds(pl.multiple_of(z * room, 16), room)

    def z_copy(source, target, send, recv, ch, i):
        return pltpu.make_async_remote_copy(
            src_ref=source.at[ch, i],
            dst_ref=target.at[ch, here],
            send_sem=send.at[ch, i],
            recv_sem=recv.at[ch, i],
            device_id={"atoms": z_dests[i]},
            device_id_type=MESH,
        )

    fronts, backs = [], []
    for ch in range(chunks):
        fronts.append([])
        backs.append([])
        for i in range(len(z_steps)):
            fill(ch, i)
            fronts[ch].append(z_copy(front, front_in, f_send, f_recv, ch, i))
            fronts[ch][i].start()
        for i in range(len(z_steps)):
            backs[ch].append(z_copy(back, back_in, b_send, b_recv, ch, i))
            backs[ch][i].start()
    last = len(z_steps)
    front_own, back_own = [], []
    for ch in range(chunks):
        fill(ch, last)
        front_own.append(pltpu.make_async_copy(front.at[ch, last], front_in.at[ch, here], f_own.at[ch]))
        back_own.append(pltpu.make_async_copy(back.at[ch, last], back_in.at[ch, here], b_own.at[ch]))
        front_own[ch].start()
        back_own[ch].start()

    def make_sign(i, carry):
        at = pl.ds(pl.multiple_of(i * 16, 16), 16)
        number = iota((16, feats), 0) + i * 16
        value = jnp.where(number == slots[0], 1.0, 0.0) - jnp.where(number == slots[1], 1.0, 0.0)
        sign[at, :] = value.astype(jnp.bfloat16)
        return carry

    lax.fori_loop(0, groups * room // 16, make_sign, 0)

    def x_copy(ch, p, k, o):
        at = every.at[pl.ds(pl.multiple_of((x * chunks + ch) * lanes + p * part, part), part), :]
        return pltpu.make_async_remote_copy(
            src_ref=at,
            dst_ref=at,
            send_sem=x_send.at[ch, p, k],
            recv_sem=x_recv.at[ch, p, k],
            device_id={"feat": lax.rem(x + o, feat_groups)},
            device_id_type=MESH,
        )

    def h_copy(k):
        return pltpu.make_async_remote_copy(
            src_ref=every.at[:HALO, k * cols : (k + 1) * cols],
            dst_ref=halo,
            send_sem=h_send.at[k],
            recv_sem=h_recv.at[0],
            device_id={"atoms": z_down, "feat": k},
            device_id_type=MESH,
        )

    def keep(ch, p, total):
        at = pl.ds(pl.multiple_of((x * chunks + ch) * lanes + p * part, part), part)
        every[at, :] = jnp.sqrt(total + 0.01)
        for k, o in enumerate(x_steps):
            x_copy(ch, p, k, o).start()

    frames, rows, blocks = frames_here, inst.shape[0], groups * reps
    me = z * reps + r
    present = ids[:, pl.ds(pl.multiple_of(z * frames, 128), frames)]
    after = ids[:, pl.ds(pl.multiple_of(jnp.minimum(z + 1, groups - 1) * frames, 128), 128)]
    after = jnp.where(z == groups - 1, -1, after)
    names = jnp.concatenate([present, after], 1).astype(jnp.float32)
    names = jnp.broadcast_to(names, (8, frames + 128))
    later = pltpu.roll(names, frames + 128 - LAG, 1)
    valid = (names == later).astype(jnp.float32)[:, :frames]
    count = jnp.sum(valid[:1], axis=1, keepdims=True)
    inverse = 1.0 / jnp.maximum(count, 1.0)
    vcol[...] = valid.T

    own = pl.ds(pl.multiple_of(x * cols, 128), cols)
    step = 32
    span = frames // (feat_groups * step)
    early = max(4 * (chunks - 1) - 1, 0)
    others_x = feat_groups - 1
    sizes = [
        feat_groups * early * step,
        (span - early + others_x * (span - 3 - early)) * step,
        others_x * 3 * step + 16,
    ]
    starts = [0, 3 * sizes[0], 3 * (sizes[0] + sizes[1])]
    sums_now[...] = jnp.zeros_like(sums_now)
    sums_next[...] = jnp.zeros_like(sums_next)

    def fold(value):
        return jnp.sum(value.reshape(step // 8, 8, value.shape[1]), 0)

    def put(stage, at, count_rows, now, later):
        size, start = sizes[stage], starts[stage]
        spot = [pl.ds(pl.multiple_of(start + n * size + at, 16), count_rows) for n in range(3)]
        high, low = split(now)
        left3[spot[0], :] = high
        left3[spot[1], :] = high
        left3[spot[2], :] = low
        right3[spot[0], :cols] = left3[spot[0], own]
        right3[spot[1], :cols] = left3[spot[2], own]
        right3[spot[2], :cols] = left3[spot[0], own]
        high, low = split(later)
        right3[spot[0], cols:] = high
        right3[spot[1], cols:] = low
        right3[spot[2], cols:] = high

    def center(ranges):
        shift[...] = jnp.zeros_like(shift)
        amount = 0
        for which, low, high in ranges:

            def add(n, carry, which=which, low=low):
                at = pl.ds(pl.multiple_of((which * span + low + n) * step, step), step)
                shift[...] = shift[...] + fold(every[at, :])
                return carry

            lax.fori_loop(0, high - low, add, 0)
            amount += (high - low) * step
        mean = jnp.sum(shift[...], 0, keepdims=True) * (1.0 / amount)
        shift[...] = jnp.broadcast_to(mean, shift.shape)

    def gather(stage, ranges):
        place = 0
        for which, low, high in ranges:

            def body(n, carry, which=which, low=low, place=place):
                base = pl.multiple_of((which * span + low + n) * step, step)
                at = pl.ds(base, step)
                weight = vcol[at, :1]
                now = (every[at, :] - shift[:1, :]) * weight
                wide = every[pl.ds(base, step + 16), own]
                moved = pltpu.roll(wide, step + 16 - LAG, 0)[:step]
                later = (moved - shift[:1, own]) * weight
                put(stage, (place + n) * step, step, now, later)
                sums_now[:8, :] = sums_now[:8, :] + fold(now)
                sums_now[8:, :] = sums_now[8:, :] + fold(now * now)
                sums_next[:8, :] = sums_next[:8, :] + fold(later)
                sums_next[8:, :] = sums_next[8:, :] + fold(later * later)
                return carry

            lax.fori_loop(0, high - low, body, 0)
            place += high - low

    def core_copy(d, b):
        return pltpu.make_async_remote_copy(
            src_ref=local.at[d, lax.rem(r + b, reps)],
            dst_ref=core.at[b - 1, d],
            send_sem=c_send.at[b - 1, d],
            recv_sem=c_recv.at[b - 1, d],
            device_id={"rep": lax.rem(r + b, reps)},
            device_id_type=MESH,
        )

    tile = max(128, reps * rows)
    tiles, inside = feats // tile, tile // (reps * rows)

    def multiply(stage, fresh, final):
        rows3 = slice(starts[stage], starts[stage] + 3 * sizes[stage])

        def body(k, carry):
            half = k // 2
            t = jnp.where(k % 2 == 0, tiles - 1 - half, half)
            at = pl.ds(pl.multiple_of(t * tile, tile), tile)
            got = lax.dot_general(
                left3[rows3, at], right3[rows3, :], (((0,), (0,)), ((), ())), preferred_element_type=jnp.float32
            )
            for j in range(inside):
                d = t * inside + j
                for b in range(reps):
                    low = (j * reps + b) * rows
                    value = got[low : low + rows]
                    local[d, b] = value if fresh else local[d, b] + value
                if final:
                    for b in range(1, reps):
                        core_copy(d, b).start()
            return carry

        lax.fori_loop(0, tiles, body, 0)

    rivals = [lax.rem(x + o, feat_groups) for o in x_steps]

    def arrived(ch, p):
        for k, o in enumerate(x_steps):
            x_copy(ch, p, k, o).wait_recv()

    def stage_early():
        for ch in range(chunks - 1):
            for p in range(2):
                arrived(ch, p)
        ranges = [(k, 0, early) for k in range(feat_groups)]
        center(ranges)
        gather(0, ranges)
        multiply(0, True, False)

    for ch in range(chunks):
        if ch == chunks - 1 and early > 0:
            stage_early()
        front_own[ch].wait()
        for copy in fronts[ch]:
            copy.wait_recv()
        delta = product(front_in[ch], sign[...], ((0,), (0,)))
        square = delta * delta
        third[...] = square[3 * part :]
        keep(ch, 0, square[:part] + square[part : 2 * part] + square[2 * part : 3 * part])
        if ch == 0:

            @pl.when(x == 0)
            def _():
                for k in range(feat_groups):
                    h_copy(k).start()

        back_own[ch].wait()
        for copy in backs[ch]:
            copy.wait_recv()
        delta = product(back_in[ch], sign[...], ((0,), (0,)))
        square = delta * delta
        keep(ch, 1, square[:part] + square[part:] + third[...])

    h_copy(0).wait_recv()
    every[frames:, own] = halo[...]
    if early == 0:
        for ch in range(chunks - 1):
            for p in range(2):
                arrived(ch, p)
    arrived(chunks - 1, 0)
    ranges = [(x, early, span)] + [(k, early, span - 3) for k in rivals]
    if early == 0:
        center(ranges)
    gather(1, ranges)
    multiply(1, early == 0, False)
    arrived(chunks - 1, 1)
    gather(2, [(k, span - 3, span) for k in rivals])
    now_off = jnp.sum(sums_now[:8, :], 0, keepdims=True) * inverse
    next_off = jnp.sum(sums_next[:8, :], 0, keepdims=True) * inverse
    root_count = jnp.sqrt(count)
    top = lax.broadcasted_iota(jnp.int32, (16, 1), 0) == 0
    now_row, next_row = now_off * root_count, next_off * root_count
    put(2, sizes[2] - 16, 16, jnp.where(top, now_row, 0.0), jnp.where(top, -next_row, 0.0))
    for n in range(3):
        spot = slice(starts[2] + (n + 1) * sizes[2] - 16, starts[2] + (n + 1) * sizes[2])
        right3[spot, :cols] = -right3[spot, :cols]
    stats[0:1, :feats] = shift[:1, :] + now_off
    stats[1:2, :feats] = jnp.maximum(
        jnp.sum(sums_now[8:, :], 0, keepdims=True) - count * now_off * now_off, 0.0
    )
    stats[2:3, :cols] = shift[:1, own] + next_off
    stats[2:3, cols : 2 * cols] = jnp.maximum(
        jnp.sum(sums_next[8:, :], 0, keepdims=True) - count * next_off * next_off, 0.0
    )
    stats[3:4, :feats] = jnp.broadcast_to(count, (1, feats))
    own_stats = pltpu.make_async_copy(stats, gathered.at[me], s_own.at[0])
    own_stats.start()
    stat_copies = []
    for k, (a, b) in enumerate(peers):
        stat_copies.append(
            pltpu.make_async_remote_copy(
                src_ref=stats,
                dst_ref=gathered.at[me],
                send_sem=s_send.at[k],
                recv_sem=s_recv.at[k],
                device_id=peer(a, b),
                device_id_type=MESH,
            )
        )
        stat_copies[-1].start()

    multiply(2, False, True)

    own_stats.wait()
    for copy in stat_copies:
        copy.wait()

    total = jnp.zeros((1, feats), jnp.float32)
    now_total = jnp.zeros((1, feats), jnp.float32)
    next_total = jnp.zeros((1, cols), jnp.float32)
    for b in range(blocks):
        size = gathered[b, 3:4, :feats]
        total = total + size
        now_total = now_total + size * gathered[b, 0:1, :feats]
        next_total = next_total + size[:, :cols] * gathered[b, 2:3, :cols]
    mean_now = now_total / total
    mean_next = next_total / total[:, :cols]
    now_spread = jnp.zeros((1, feats), jnp.float32)
    next_spread = jnp.zeros((1, cols), jnp.float32)
    for b in range(blocks):
        size = gathered[b, 3:4, :feats]
        off = gathered[b, 0:1, :feats] - mean_now
        now_spread = now_spread + (gathered[b, 1:2, :feats] + size * off * off)
        off = gathered[b, 2:3, :cols] - mean_next
        next_spread = next_spread + (gathered[b, 2:3, cols : 2 * cols] + size[:, :cols] * off * off)
    scale_now = 1.0 / jnp.sqrt(now_spread / total + 1e-05)
    scale_next = 1.0 / jnp.sqrt(next_spread / total[:, :cols] + 1e-05)
    root = 1.0 / jnp.sqrt(total)
    table[blocks : blocks + 1, :] = scale_now * root
    table[blocks + 1 : blocks + 2, :] = mean_now
    table[blocks + 2 : blocks + 3, :] = scale_now
    table[blocks + 3 :, :] = jnp.zeros((5, feats), jnp.float32)
    for b in range(blocks):
        size = gathered[b, 3:4, :feats]
        table[b : b + 1, :] = (gathered[b, 0:1, :feats] - mean_now) * (scale_now * root)
        side[b : b + 1, cols:] = (
            size[:, :cols] * (gathered[b, 2:3, :cols] - mean_next) * (scale_next * root[:, :cols])
        )
    for b in range(blocks):
        side[b : b + 1, :cols] = gathered[b, 3:4, :cols] * table[b : b + 1, own]
    scales[0:1, :cols] = table[blocks : blocks + 1, own]
    scales[0:1, cols:] = scale_next * root[:, :cols]
    columns[...] = table[...].T

    tall = min(rows // PIECES, 32)
    piece = rows // PIECES

    def hop(d, s, up):
        at = pl.ds(pl.multiple_of(s * piece, piece), piece)
        return pltpu.make_async_remote_copy(
            src_ref=sums.at[d, at],
            dst_ref=(from_below if up else from_above).at[d, at],
            send_sem=z_send.at[d, s],
            recv_sem=(l_recv if up else r_recv).at[d, s],
            device_id={"atoms": lax.rem(z + (1 if up else groups - 1), groups)},
            device_id_type=MESH,
        )

    def mine(d, i):
        at = pl.ds(pl.multiple_of(i * tall, tall), tall)
        value = local[d, r, at, :]
        for b in range(1, reps):
            value = value + core[b - 1, d, at, :]
        high = pl.ds(pl.multiple_of((d * reps + r) * rows + i * tall, tall), tall)
        return value * columns[high, blocks : blocks + 1] * scales[0:1, :]

    def wait_core(d):
        for b in range(1, reps):
            core_copy(d, b).wait_recv()

    def send(d, s, up, relay):
        if relay:
            hop(d, s, up).wait_recv()

        def body(j, carry):
            i = s * (piece // tall) + j
            at = pl.ds(pl.multiple_of(i * tall, tall), tall)
            value = mine(d, i)
            inst_part, lag_part = value[:, :cols], value[:, cols:]
            if relay:
                more = decode((from_below if up else from_above)[d, at, :])
                inst_part, lag_part = inst_part + more[0], lag_part + more[1]
            sums[d, at, :] = encode(inst_part, lag_part)
            return carry

        lax.fori_loop(0, piece // tall, body, 0)
        hop(d, s, up).start()

    turn_above = PIECES * z
    turn_below = PIECES * (groups - 1 - z) + jnp.where(z >= groups // 2, 1, 0)

    def chain(turn, carry):
        down, up = turn - turn_below, turn - turn_above

        @pl.when((down >= 0) & (down < PIECES * z))
        def _():
            below, s = down // PIECES, down % PIECES

            @pl.when(s == 0)
            def _():
                wait_core(below)

            @pl.when(z == groups - 1)
            def _():
                send(below, s, False, False)

            @pl.when(z < groups - 1)
            def _():
                send(below, s, False, True)

        @pl.when((up >= 0) & (up < PIECES * (groups - 1 - z)))
        def _():
            above, s = groups - 1 - up // PIECES, up % PIECES

            @pl.when(s == 0)
            def _():
                wait_core(above)

            @pl.when(z == 0)
            def _():
                send(above, s, True, False)

            @pl.when(z > 0)
            def _():
                send(above, s, True, True)

        return carry

    lax.fori_loop(0, PIECES * (groups - 1) + 1, chain, 0)

    wait_core(z)

    def settle(i, carry):
        at = pl.ds(pl.multiple_of(i * tall, tall), tall)
        high = pl.ds(pl.multiple_of(me * rows + i * tall, tall), tall)
        shift = lax.dot_general(
            columns[high, :blocks], side[...], (((1,), (0,)), ((), ())),
            precision=lax.Precision.HIGHEST, preferred_element_type=jnp.float32,
        )
        value = mine(z, i) + shift
        inst[at, :] = value[:, :cols]
        lag[at, :] = value[:, cols:]
        return carry

    lax.fori_loop(0, rows // tall, settle, 0)

    middle, stretch = table[blocks + 1 : blocks + 2, own], table[blocks + 2 : blocks + 3, own]

    def project(i, carry):
        at = pl.ds(pl.multiple_of(i * step, step), step)
        proj[at, :] = (every[at, own] - middle) * stretch
        return carry

    lax.fori_loop(0, frames // step, project, 0)

    def arrive(up):
        def body(s, carry):
            hop(z, s, up).wait_recv()
            at = pl.ds(pl.multiple_of(s * piece, piece), piece)
            more = decode((from_below if up else from_above)[z, at, :])
            inst[at, :] = inst[at, :] + more[0]
            lag[at, :] = lag[at, :] + more[1]
            return carry

        lax.fori_loop(0, PIECES, body, 0)

    @pl.when(z > 0)
    def _():
        arrive(True)

    @pl.when(z < groups - 1)
    def _():
        arrive(False)

    def finish(d, carry):
        for b in range(1, reps):
            core_copy(d, b).wait_send()

        @pl.when(z < d)
        def _():
            for s in range(PIECES):
                hop(d, s, True).wait_send()

        @pl.when(z > d)
        def _():
            for s in range(PIECES):
                hop(d, s, False).wait_send()

        return carry

    lax.fori_loop(0, groups, finish, 0)

    @pl.when(x == 0)
    def _():
        for k in range(feat_groups):
            h_copy(k).wait_send()

    for ch in range(chunks):
        for copy in fronts[ch] + backs[ch]:
            copy.wait_send()
        for p in range(2):
            for k, o in enumerate(x_steps):
                x_copy(ch, p, k, o).wait_send()


def program(coords, pairs, ids, room, groups, feat_groups, reps):
    cols, width = pairs.shape[1], coords.shape[2]
    feats, frames = cols * feat_groups, coords.shape[1] // groups
    chunks = frames // (feat_groups * 128)
    height = -(-groups * -(-width // 128) // 16) * 16
    blocks = groups * reps
    rows = feats // blocks
    vmem = pl.BlockSpec(memory_space=pltpu.VMEM)
    z_count, x_count, core_count = max(groups - 1, 1), max(feat_groups - 1, 1), max(reps - 1, 1)
    others = max(blocks - 1, 1)
    dma = pltpu.SemaphoreType.DMA
    bf16, f32, i32 = jnp.bfloat16, jnp.float32, jnp.int32
    memory = [
        ((frames + HALO, feats), f32),
        ((HALO, cols), f32),
        ((chunks, groups, 3, 128, width), bf16),
        ((feat_groups, 2, cols), i32),
        ((height, 128), f32),
        ((room, width), bf16),
        ((chunks, groups, room, 256), bf16),
        ((chunks, groups, room, 128), bf16),
        ((groups * room, feats), bf16),
        ((chunks, groups * room, 256), bf16),
        ((chunks, groups * room, 128), bf16),
        ((64, feats), f32),
        ((8, feats), f32),
        ((16, feats), f32),
        ((16, cols), f32),
        ((frames, 8), f32),
        ((3 * frames + 48, feats), bf16),
        ((3 * frames + 48, 2 * cols), bf16),
        ((groups, reps, rows, 2 * cols), f32),
        ((core_count, groups, rows, 2 * cols), f32),
        ((4, max(feats, 2 * cols)), f32),
        ((blocks, 4, max(feats, 2 * cols)), f32),
        ((blocks + 8, feats), f32),
        ((blocks, 2 * cols), f32),
        ((feats, blocks + 8), f32),
        ((8, 2 * cols), f32),
        ((groups, rows, cols), i32),
        ((groups, rows, cols), i32),
        ((groups, rows, cols), i32),
    ]
    signals = [
        (chunks, groups),
        (x_count,),
        (x_count,),
        (chunks, z_count),
        (chunks, z_count),
        (chunks, z_count),
        (chunks, z_count),
        (chunks,),
        (chunks,),
        (chunks, 2, x_count),
        (chunks, 2, x_count),
        (feat_groups,),
        (1,),
        (core_count, groups),
        (core_count, groups),
        (1,),
        (others,),
        (others,),
        (groups, PIECES),
        (groups, PIECES),
        (groups, PIECES),
    ]
    return pl.pallas_call(
        functools.partial(program_kernel, groups, feat_groups, reps, room, chunks),
        out_shape=(
            jax.ShapeDtypeStruct((rows, cols), f32),
            jax.ShapeDtypeStruct((rows, cols), f32),
            jax.ShapeDtypeStruct((frames, cols), f32),
            jax.ShapeDtypeStruct((1, 1), f32),
        ),
        in_specs=[pl.BlockSpec(memory_space=pl.ANY), vmem, vmem],
        out_specs=(vmem, vmem, vmem, pl.BlockSpec(memory_space=pltpu.SMEM)),
        scratch_shapes=[pltpu.VMEM(*m) for m in memory] + [dma(m) for m in signals],
        compiler_params=pltpu.CompilerParams(
            collective_id=0, has_side_effects=True, vmem_limit_bytes=60 * 1024 * 1024
        ),
    )(coords, pairs, ids)


def encode(inst, lag):
    def one(v):
        root = v * lax.rsqrt(jnp.abs(v) + 1e-30)
        return jnp.round(root * CODE).astype(jnp.int32)

    return (one(inst) << 16) | (one(lag) & 0xFFFF)


def decode(word):
    def one(q):
        root = q.astype(jnp.float32) * (1.0 / CODE)
        return root * jnp.abs(root)

    return one(word >> 16), one((word << 16) >> 16)


def split(value):
    high = value.astype(jnp.bfloat16)
    return high, (value - high.astype(jnp.float32)).astype(jnp.bfloat16)


def write_kernel(*refs):
    count = len(refs) // 2
    ins, outs, sem = refs[:count], refs[count:-1], refs[-1]
    copies = [pltpu.make_async_copy(a, b, sem.at[i]) for i, (a, b) in enumerate(zip(ins, outs))]
    for copy in copies:
        copy.start()
    for copy in copies:
        copy.wait()


def write_out(*arrays):
    vmem, anywhere = pl.BlockSpec(memory_space=pltpu.VMEM), pl.BlockSpec(memory_space=pl.ANY)
    return pl.pallas_call(
        write_kernel,
        out_shape=tuple(jax.ShapeDtypeStruct(a.shape, a.dtype) for a in arrays),
        in_specs=[vmem] * len(arrays),
        out_specs=(anywhere,) * len(arrays),
        scratch_shapes=[pltpu.SemaphoreType.DMA((len(arrays),))],
    )(*arrays)


def slots_per_pass(width, refs, atoms):
    share = width * (1.0 - math.exp(-refs / atoms)) + 1.5 * math.sqrt(width)
    return min(-(-width // 16) * 16, -(-int(share) // 16) * 16)


def collect(value, axis):
    size = lax.axis_size(axis)
    return lax.all_to_all(jnp.broadcast_to(value[None], (size,) + value.shape), axis, 0, 0, tiled=True)


def plain(coords, atom_pairs, traj_ids):
    groups, feat_groups, reps = lax.axis_size("atoms"), lax.axis_size("feat"), lax.axis_size("rep")
    z, x = lax.axis_index("atoms"), lax.axis_index("feat")
    width, cols = coords.shape[2], atom_pairs.shape[1]
    frames = coords.shape[1] // groups
    feats = cols * feat_groups
    exact = lax.Precision.HIGHEST

    split_up = jnp.transpose(coords.reshape(3, groups, frames, width), (1, 0, 2, 3))
    got = lax.all_to_all(split_up, "atoms", 0, 0, tiled=True)
    number = jnp.arange(groups * width, dtype=jnp.int32)[:, None]
    sign = (number == atom_pairs[0]).astype(jnp.bfloat16) - (number == atom_pairs[1]).astype(jnp.bfloat16)
    delta = matmul(got, sign.reshape(groups, width, cols), ((0, 3), (0, 1)))
    own = jnp.sqrt(jnp.sum(delta * delta, 0) + 0.01)
    every = jnp.transpose(collect(own, "feat"), (1, 0, 2)).reshape(frames, feats)
    incoming = lax.ppermute(own[:LAG], "atoms", [(i, (i - 1) % groups) for i in range(groups)])
    future = jnp.concatenate([own[LAG:], incoming], 0)
    ids = jnp.concatenate([traj_ids[0], jnp.full((LAG,), -1, jnp.int32)])
    now = lax.dynamic_slice_in_dim(ids, z * frames, frames)
    later = lax.dynamic_slice_in_dim(ids, z * frames + LAG, frames)
    valid = (now == later).astype(jnp.float32)[:, None]

    def total(value):
        return jnp.sum(collect(jnp.sum(collect(value, "rep"), 0), "atoms"), 0)

    count = total(jnp.full((128,), jnp.sum(valid)))[0]
    mean_now = total(jnp.sum(valid * every, 0)) / count
    mean_next = total(jnp.sum(valid * future, 0)) / count
    now_c, next_c = valid * (every - mean_now), valid * (future - mean_next)
    scale_now = 1.0 / jnp.sqrt(total(jnp.sum(now_c * now_c, 0)) / count + 1e-05)
    scale_next = 1.0 / jnp.sqrt(total(jnp.sum(next_c * next_c, 0)) / count + 1e-05)
    own_c = lax.dynamic_slice_in_dim(now_c, x * cols, cols, 1)
    own_scale = lax.dynamic_slice_in_dim(scale_now, x * cols, cols)
    own_mean = lax.dynamic_slice_in_dim(mean_now, x * cols, cols)
    local = matmul(now_c, jnp.concatenate([own_c, next_c], 1), ((0,), (0,)), exact)
    rows = feats // (groups * reps)
    local = local.reshape(groups, reps, rows, 2 * cols)
    local = jnp.sum(lax.all_to_all(local, "atoms", 0, 0, tiled=True), 0)
    mine = jnp.sum(lax.all_to_all(local, "rep", 0, 0, tiled=True), 0)
    row = (z * reps + lax.axis_index("rep")) * rows
    scale_rows = lax.dynamic_slice_in_dim(scale_now, row, rows)[:, None]
    corr_inst = mine[:, :cols] / count * scale_rows * own_scale
    corr_lag = mine[:, cols:] / count * scale_rows * scale_next
    return corr_inst, corr_lag, (own - own_mean) * own_scale


def shards(atom_coords, atom_pairs, traj_ids):
    groups, feat_groups, reps = lax.axis_size("atoms"), lax.axis_size("feat"), lax.axis_size("rep")
    width = atom_coords.shape[3]
    room = slots_per_pass(width, 2 * atom_pairs.shape[1] * feat_groups, width * groups)
    coords = jnp.transpose(atom_coords[0], (1, 0, 2))
    *results, over = program(coords, atom_pairs, traj_ids, room, groups, feat_groups, reps)
    corr_inst, corr_lag, projections = lax.cond(
        over[0, 0] > room,
        lambda a: plain(coords, atom_pairs, traj_ids),
        lambda a: write_out(*a),
        results,
    )
    return (corr_inst, corr_lag, projections[None])


def solution(mesh):
    placed = (P(("grp", "rep"), None, None, "atoms"), P(None, "feat"), P(("grp", "rep"), None))
    return jax.shard_map(
        shards,
        mesh=mesh,
        in_specs=placed,
        out_specs=(
            P(("grp", "atoms", "rep"), "feat"),
            P(("grp", "atoms", "rep"), "feat"),
            P(("grp", "rep"), "atoms", "feat"),
        ),
        check_vma=False,
    )
```
